128 devices in a mesh: row: 8 (over z, y_hi), col: 16 (over x, y_lo, core).
Axes of the slice: x: 4, y: 4 (y_hi: 2, y_lo: 2; y = y_hi * 2 + y_lo), z: 4, core: 2. Of those that a mesh axis runs over, the one named last changes fastest.
Arguments:
- tokens: bfloat16 [1536, 14336], P('col', 'row'), may hold values from -6 to 6
- weight_in: bfloat16 [14336, 14336], P('row', 'col'), may hold values from -0.046875 to 0.046875
- bias_hidden: float32 [14336], P('col'), may hold values from -3 to 3
- weight_out: bfloat16 [14336, 14336], P('col', 'row'), may hold values from -0.046875 to 0.046875
- out_grad: bfloat16 [1536, 14336], P('col', 'row'), may hold values from -0.75 to 0.75
Outputs:
- grad_tokens: bfloat16 [1536, 14336], P('col', 'row')
- grad_weight_in: float32 [14336, 14336], P('row', 'col')
- grad_bias: float32 [14336], P('col')
- grad_weight_out: float32 [14336, 14336], P('col', 'row')
The draws below stay inside these ranges and needn't reach their ends.
All inputs are finite; a program needn't handle non-finite values.
Results may differ from the reference program's by a relative error of at most 0.007.
Values may be sent and summed in bfloat16 or wider, within the bound.
A program may use at most 128 MiB of HBM per device.

```python
import jax
import jax.numpy as jnp
from jax import lax

D = 14336
FFC = 14336
TOKENS = 1536


def shard_levels(stream_key, dims, shards, least, high):
    gain, own = 1.0, jax.random.fold_in(stream_key, 6)
    for axis_at, shards_of in shards:
        draws = jnp.exp(jax.random.uniform(jax.random.fold_in(own, axis_at), (shards_of,), jnp.float32, least / len(shards), high / len(shards)))
        gain = gain * jnp.repeat(draws, dims[axis_at] // shards_of).reshape([-1 if axis == axis_at else 1 for axis in range(len(dims))])
    return gain


def noise(stream_key, dims, scale, reach, split=(), kind=jnp.bfloat16):
    values = scale * jax.random.normal(stream_key, dims, jnp.float32)
    if split:
        values = values * shard_levels(stream_key, dims, split, -0.22, 0.18)
    return jnp.clip(values, -reach, reach).astype(kind)


def setup_inputs(seed: int = 0) -> dict:
    streams_of = jax.random.split(jax.random.key(seed), 6)
    return {
        "tokens": noise(streams_of[0], (TOKENS, D), 1.0, 6.0, ((0, 16), (1, 8))),
        "weight_in": noise(streams_of[1], (D, FFC), D ** -0.5, 0.046875, ((0, 8), (1, 16))),
        "bias_hidden": noise(streams_of[2], (FFC,), 0.5, 3.0, ((0, 16),), jnp.float32),
        "weight_out": noise(streams_of[3], (FFC, D), FFC ** -0.5, 0.046875, ((0, 16), (1, 8))),
        "out_grad": noise(streams_of[4], (TOKENS, D), 0.125, 0.75, ((0, 16), (1, 8))),
    }


GELU_SCALE = 0.7978845608
GELU_CUBIC = 0.044715


def gelu_parts(values):
    inner = GELU_SCALE * (values + GELU_CUBIC * values * values * values)
    tangent = jnp.tanh(inner)
    result = 0.5 * values * (1.0 + tangent)
    slope = 0.5 * (1.0 + tangent) + 0.5 * values * (1.0 - tangent * tangent) * GELU_SCALE * (1.0 + 3.0 * GELU_CUBIC * values * values)
    return result, slope


def contract_rows(left, right):
    return lax.dot_general(left, right, (((0,), (0,)), ((), ())), preferred_element_type=jnp.float32)


def reference(tokens, weight_in, bias_hidden, weight_out, out_grad):
    pre = jnp.dot(tokens, weight_in, preferred_element_type=jnp.float32) + bias_hidden
    act_grad = lax.dot_general(out_grad, weight_out, (((1,), (1,)), ((), ())), preferred_element_type=jnp.float32)
    result, slope = gelu_parts(pre)
    act = result.astype(jnp.bfloat16)
    pre_grad = (act_grad * slope).astype(jnp.bfloat16)
    grad_bias = jnp.sum(pre_grad, axis=0, dtype=jnp.float32)
    grad_weight_out = contract_rows(act, out_grad)
    grad_weight_in = contract_rows(tokens, pre_grad)
    grad_tokens = lax.dot_general(pre_grad, weight_in, (((1,), (1,)), ((), ())), preferred_element_type=jnp.float32).astype(jnp.bfloat16)
    return grad_tokens, grad_weight_in, grad_bias, grad_weight_out
```

```python
import jax
import jax.numpy as jnp
from jax import lax
from jax.experimental import pallas as pl
from jax.experimental.pallas import tpu as pltpu
from jax.sharding import PartitionSpec as P

GELU_SCALE = 0.7978845608
GELU_CUBIC = 0.044715
MESH = pl.DeviceIdType.MESH
BF16 = jnp.bfloat16
F32 = jnp.float32

CHUNKS = ((0, 0), (1, 0), (3, 0), (2, 0), (2, 1), (1, 1), (3, 1), (0, 1))
SLOT = {where: at for at, where in enumerate(CHUNKS)}
N_CHUNKS = len(CHUNKS)
N_MESSAGES = 192


def gelu_parts(values):
    inner = GELU_SCALE * (values + GELU_CUBIC * values * values * values)
    tangent = jnp.tanh(inner)
    result = 0.5 * values * (1.0 + tangent)
    slope = 0.5 * (1.0 + tangent) + 0.5 * values * (1.0 - tangent * tangent) * GELU_SCALE * (
        1.0 + 3.0 * GELU_CUBIC * values * values
    )
    return (result, slope)


def dot_nn(left, right):
    return lax.dot_general(left, right, (((1,), (0,)), ((), ())), preferred_element_type=F32)


def dot_nt(left, right):
    return lax.dot_general(left, right, (((1,), (1,)), ((), ())), preferred_element_type=F32)


def dot_tn(left, right):
    return lax.dot_general(left, right, (((0,), (0,)), ((), ())), preferred_element_type=F32)


def tiles(total, size):
    return [(at, min(size, total - at)) for at in range(0, total, size)]


def exchange_kernel(
    tok_h, win_h, bias, wout_h, og_h,
    gt, tok_o, og_o, act_o, pg_o,
    win, wout, tok, og, act, pg, part, r1, r2, comb, summed, summed_in,
    g_out, g_in, keep, keep_in, x2_out, x2_in, x1_out, x1_in,
    send_sem, recv_sem, local_sem,
):
    own, dm = tok_h.shape
    ff = win.shape[1]
    piece = 2 * own // 4
    half = dm // 2
    row, col = lax.axis_index("row"), lax.axis_index("col")
    z, yh = row // 2, row % 2
    x, yl, core = col // 4, (col // 2) % 2, col % 2

    def device(z_, yh_, x_, yl_, core_):
        return (z_ * 2 + yh_, (x_ * 2 + yl_) * 2 + core_)

    to_sib = device(z, yh, x, yl, 1 - core)
    to_yl = device(z, yh, x, 1 - yl, core)
    to_yh = device(z, 1 - yh, x, yl, core)
    to_xp, to_xm = device(z, yh, (x + 1) % 4, yl, core), device(z, yh, (x + 3) % 4, yl, core)
    to_zp, to_zm = device((z + 1) % 4, yh, x, yl, core), device((z + 3) % 4, yh, x, yl, core)
    z1, z2, z3 = (z + 1) % 4, (z + 2) % 4, (z + 3) % 4

    def rows(at):
        return pl.ds(pl.multiple_of(at * piece, piece), piece)

    copies = []

    def send(src, dst, target):
        at = len(copies)
        copy = pltpu.make_async_remote_copy(
            src_ref=src, dst_ref=dst, send_sem=send_sem.at[at], recv_sem=recv_sem.at[at],
            device_id=target, device_id_type=MESH,
        )
        copy.start()
        copies.append(copy)
        return copy

    locals_ = []

    def local_copy(src, dst):
        copy = pltpu.make_async_copy(src, dst, local_sem.at[len(locals_)])
        copy.start()
        locals_.append(copy)
        return copy

    barrier = pltpu.get_barrier_semaphore()
    for target in (to_sib, to_yl, to_yh, to_xp, to_xm, to_zp, to_zm):
        pl.semaphore_signal(barrier, inc=1, device_id=target, device_id_type=MESH)

    mine, other = pl.ds(0, own), pl.ds(own, own)
    load_tok = local_copy(tok_h, tok.at[0, mine])
    load_win = local_copy(win_h, win)
    load_og = local_copy(og_h, og.at[0, mine])
    load_wout = local_copy(wout_h, wout)
    pl.semaphore_wait(barrier, 7)

    gather = {}
    pairs = ((0, tok_h, tok), (1, og_h, og))
    for a, src, buf in pairs:
        gather[a, 0, "s"] = send(src, buf.at[0, other], to_sib)
        gather[a, SLOT[0, 1]] = send(src, buf.at[SLOT[0, 1], mine], to_yl)
        gather[a, SLOT[3, 0]] = send(src, buf.at[SLOT[3, 0], mine], to_xp)
        gather[a, SLOT[1, 0]] = send(src, buf.at[SLOT[1, 0], mine], to_xm)

    def buf_of(a):
        return (tok, og)[a]

    def relay_to_sibling(a, k):
        gather[a, k].wait_recv()
        buf = buf_of(a)
        gather[a, k, "s"] = send(buf.at[k, mine], buf.at[k, other], to_sib)

    def relay_far(dy):
        far = SLOT[2, dy]
        gather[0, far] = send(tok.at[SLOT[3, dy], mine], tok.at[far, mine], to_xp)
        gather[1, far] = send(og.at[SLOT[1, dy], mine], og.at[far, mine], to_xm)

    def relay_pair(a):
        buf, k = buf_of(a), SLOT[0, 1]
        gather[a, SLOT[3, 1]] = send(buf.at[k, mine], buf.at[SLOT[3, 1], mine], to_xp)
        gather[a, SLOT[1, 1]] = send(buf.at[k, mine], buf.at[SLOT[1, 1], mine], to_xm)

    red = {}

    def partial_pre(k):
        gather[0, k, "s"].wait_recv()
        if k == 0:
            load_tok.wait()
            load_win.wait()
        for at, size in tiles(ff, 256):
            part[k, 0, :, at : at + size] = dot_nn(tok[k], win[:, at : at + size]).astype(BF16)
        red[k, "1p"] = send(part.at[k, 0, rows(z2)], r1.at[k, 0], to_zp)
        red[k, "2pm"] = send(part.at[k, 0, rows(z3)], r2.at[k, 1], to_zm)
        local_copy(tok.at[k], tok_o.at[k])

    def partial_act(k):
        gather[1, k, "s"].wait_recv()
        if k == 0:
            load_og.wait()
            load_wout.wait()
        for at, size in tiles(ff, 256):
            part[k, 1, :, at : at + size] = dot_nt(og[k], wout[at : at + size, :]).astype(BF16)
        red[k, "1a"] = send(part.at[k, 1, rows(z2)], r1.at[k, 1], to_zm)
        red[k, "2ap"] = send(part.at[k, 1, rows(z1)], r2.at[k, 2], to_zp)
        local_copy(og.at[k], og_o.at[k])

    def combine(k):
        red[k, "1p"].wait_recv()
        comb[k, 0] = (part[k, 0, rows(z1), :].astype(F32) + r1[k, 0].astype(F32)).astype(BF16)
        red[k, "2pp"] = send(comb.at[k, 0], r2.at[k, 0], to_zp)
        red[k, "1a"].wait_recv()
        comb[k, 1] = (part[k, 1, rows(z3), :].astype(F32) + r1[k, 1].astype(F32)).astype(BF16)
        red[k, "2am"] = send(comb.at[k, 1], r2.at[k, 3], to_zm)

    def reduce_pair(k):
        for name in ("2pm", "2ap", "2pp", "2am"):
            red[k, name].wait_recv()
        for a in range(2):
            total = part[k, a, rows(z), :].astype(F32) + (r2[k, 2 * a].astype(F32) + r2[k, 2 * a + 1].astype(F32))
            summed[k, a] = total.astype(BF16)
        red[k, "y"] = send(summed.at[k], summed_in.at[k], to_yh)

    def activate(k):
        red[k, "y"].wait_recv()
        pre = summed[k, 0].astype(F32) + summed_in[k, 0].astype(F32) + bias[...]
        act_grad = summed[k, 1].astype(F32) + summed_in[k, 1].astype(F32)
        result, slope = gelu_parts(pre)
        act[k, rows(z), :] = result.astype(BF16)
        pg[k, rows(z), :] = (act_grad * slope).astype(BF16)
        here = rows(z)
        red[k, "gpp"] = send(pg.at[k, here], pg.at[k, here], to_zp)
        red[k, "gpm"] = send(pg.at[k, here], pg.at[k, here], to_zm)
        red[k, "gap"] = send(act.at[k, here], act.at[k, here], to_zp)
        red[k, "gam"] = send(act.at[k, here], act.at[k, here], to_zm)

    def spread(k):
        red[k, "gpm"].wait_recv()
        red[k, "fp"] = send(pg.at[k, rows(z1)], pg.at[k, rows(z1)], to_zm)
        red[k, "gap"].wait_recv()
        red[k, "fa"] = send(act.at[k, rows(z3)], act.at[k, rows(z3)], to_zp)

    back = {}

    def grad_in(k):
        for name in ("gpp", "fp"):
            red[k, name].wait_recv()
        local_copy(pg.at[k], pg_o.at[k])
        for at, size in tiles(dm, 256):
            product = dot_nt(pg[k], win[at : at + size, :])
            keep[k, :, at : at + size] = product[:own].astype(BF16)
            g_out[k, :, at : at + size] = product[own:].astype(BF16)
        back[k, "s"] = send(g_out.at[k], g_in.at[k], to_sib)

    def store_act(k):
        for name in ("gam", "fa"):
            red[k, name].wait_recv()
        local_copy(act.at[k], act_o.at[k])

    def join_cores(k):
        back[k, "s"].wait_recv()
        dx, dy = CHUNKS[k]
        keep[k] = (keep[k].astype(F32) + g_in[k].astype(F32)).astype(BF16)
        if dy:
            back[dx, "y"] = send(keep.at[k], keep_in.at[dx], to_yl)

    def joined(dx, side):
        cols = pl.ds(side * half, half)
        return keep[SLOT[dx, 0], :, cols].astype(F32) + keep_in[dx, :, cols].astype(F32)

    def return_far():
        back[2, "y"].wait_recv()
        for side in range(2):
            x2_out[side] = joined(2, side).astype(BF16)
        back["far", 0] = send(x2_out.at[0], x2_in.at[0], to_xp)
        back["far", 1] = send(x2_out.at[1], x2_in.at[1], to_xm)

    def return_near(dx):
        way, target = (0, to_xp) if dx == 1 else (1, to_xm)
        back[dx, "y"].wait_recv()
        x1_out[way, 1 - way] = joined(dx, 1 - way).astype(BF16)
        back["near", way, 1 - way] = send(x1_out.at[way, 1 - way], x1_in.at[way, 1 - way], target)
        back["far", way].wait_recv()
        x1_out[way, way] = (joined(dx, way) + x2_in[way].astype(F32)).astype(BF16)
        back["near", way, way] = send(x1_out.at[way, way], x1_in.at[way, way], target)

    def finish():
        back[0, "y"].wait_recv()
        for side in range(2):
            for way in range(2):
                back["near", way, side].wait_recv()
            total = joined(0, side) + (x1_in[0, side].astype(F32) + x1_in[1, side].astype(F32))
            gt[:, side * half : (side + 1) * half] = total.astype(BF16)

    def relays_first():
        for a in range(2):
            for k in (SLOT[1, 0], SLOT[3, 0]):
                relay_to_sibling(a, k)
        relay_far(0)
        for a in range(2):
            relay_to_sibling(a, SLOT[0, 1])
            relay_pair(a)

    def relays_second():
        for a in range(2):
            relay_to_sibling(a, SLOT[2, 0])

    def relays_third():
        for a in range(2):
            for k in (SLOT[1, 1], SLOT[3, 1]):
                relay_to_sibling(a, k)
        relay_far(1)

    def relays_fourth():
        for a in range(2):
            relay_to_sibling(a, SLOT[2, 1])

    def at(stage, k):
        if 0 <= k < N_CHUNKS:
            stage(k)

    partial_pre(0)
    partial_act(0)
    combine(0)
    reduce_pair(0)
    relays_first()
    for t in range(1, N_CHUNKS + 7):
        if t == 1:
            activate(0)
        if t == 2:
            relays_second()
        if t == 3:
            relays_third()
        if t == 4:
            relays_fourth()
        if t > 1:
            at(combine, t - 1)
        at(partial_pre, t)
        at(partial_act, t)
        if t > 2:
            at(activate, t - 2)
        at(spread, t - 3)
        at(grad_in, t - 4)
        at(store_act, t - 4)
        at(join_cores, t - 5)
        if t - 6 == SLOT[2, 1]:
            return_far()
        if t - 6 == SLOT[1, 1]:
            return_near(1)
        if t - 6 == SLOT[3, 1]:
            return_near(3)
        if t > 1:
            at(reduce_pair, t - 1)
    finish()
    for copy in copies:
        copy.wait_send()
    for copy in locals_[4:]:
        copy.wait()


def exchange(tokens, weight_in, bias_hidden, weight_out, out_grad):
    own, dm = tokens.shape
    ff = weight_in.shape[1]
    chunk, piece, half = 2 * own, own // 2, dm // 2
    n = N_CHUNKS
    any_space = pl.BlockSpec(memory_space=pl.ANY)
    vmem = pl.BlockSpec(memory_space=pltpu.VMEM)
    flops = 3 * 2 * n * chunk * dm * ff
    return pl.pallas_call(
        exchange_kernel,
        out_shape=(
            jax.ShapeDtypeStruct((own, dm), BF16),
            jax.ShapeDtypeStruct((n, chunk, dm), BF16),
            jax.ShapeDtypeStruct((n, chunk, dm), BF16),
            jax.ShapeDtypeStruct((n, chunk, ff), BF16),
            jax.ShapeDtypeStruct((n, chunk, ff), BF16),
        ),
        in_specs=[any_space, any_space, vmem, any_space, any_space],
        out_specs=(vmem, any_space, any_space, any_space, any_space),
        scratch_shapes=[
            pltpu.VMEM((dm, ff), BF16),
            pltpu.VMEM((ff, dm), BF16),
            pltpu.VMEM((n, chunk, dm), BF16),
            pltpu.VMEM((n, chunk, dm), BF16),
            pltpu.VMEM((n, chunk, ff), BF16),
            pltpu.VMEM((n, chunk, ff), BF16),
            pltpu.VMEM((n, 2, chunk, ff), BF16),
            pltpu.VMEM((n, 2, piece, ff), BF16),
            pltpu.VMEM((n, 4, piece, ff), BF16),
            pltpu.VMEM((n, 2, piece, ff), BF16),
            pltpu.VMEM((n, 2, piece, ff), BF16),
            pltpu.VMEM((n, 2, piece, ff), BF16),
            pltpu.VMEM((n, own, dm), BF16),
            pltpu.VMEM((n, own, dm), BF16),
            pltpu.VMEM((n, own, dm), BF16),
            pltpu.VMEM((4, own, dm), BF16),
            pltpu.VMEM((2, own, half), BF16),
            pltpu.VMEM((2, own, half), BF16),
            pltpu.VMEM((2, 2, own, half), BF16),
            pltpu.VMEM((2, 2, own, half), BF16),
            pltpu.SemaphoreType.DMA((N_MESSAGES,)),
            pltpu.SemaphoreType.DMA((N_MESSAGES,)),
            pltpu.SemaphoreType.DMA((4 + 4 * n,)),
        ],
        compiler_params=pltpu.CompilerParams(
            collective_id=0, has_side_effects=True, vmem_limit_bytes=60 * 1024 * 1024
        ),
        cost_estimate=pl.CostEstimate(flops=flops, bytes_accessed=40_000_000, transcendentals=0),
        name="exchange",
    )(tokens, weight_in, bias_hidden.reshape(1, ff), weight_out, out_grad)


def local(tokens, weight_in, bias_hidden, weight_out, out_grad):
    grad_tokens, tok_all, grad_all, act_all, pre_grad_all = exchange(
        tokens, weight_in, bias_hidden, weight_out, out_grad
    )
    flat = lambda array: array.reshape(-1, array.shape[-1])
    tok_all, grad_all, act_all, pre_grad_all = map(flat, (tok_all, grad_all, act_all, pre_grad_all))
    grad_bias = jnp.sum(pre_grad_all, axis=0, dtype=F32)
    grad_weight_out = dot_tn(act_all, grad_all)
    grad_weight_in = dot_tn(tok_all, pre_grad_all)
    return (grad_tokens, grad_weight_in, grad_bias, grad_weight_out)


def solution(mesh):
    placed = (P("col", "row"), P("row", "col"), P("col"), P("col", "row"), P("col", "row"))
    return jax.shard_map(
        local,
        mesh=mesh,
        in_specs=placed,
        out_specs=(P("col", "row"), P("row", "col"), P("col"), P("col", "row")),
        check_vma=False,
    )
```

```python
import jax
import jax.numpy as jnp
from jax import lax
from jax.experimental import pallas as pl
from jax.experimental.pallas import tpu as pltpu
from jax.sharding import PartitionSpec as P

GELU_SCALE = 0.7978845608
GELU_CUBIC = 0.044715
MESH = pl.DeviceIdType.MESH
BF16 = jnp.bfloat16
F32 = jnp.float32

CHUNKS = ((0, 0), (1, 0), (1, 1), (3, 0), (3, 1), (2, 0), (0, 1), (2, 1))
SCHEDULE = (
    ("start",), ("load",), ("pre", 0), ("actp", 0), ("combp", 0), ("comba", 0), ("rel", 0, 3), ("rel", 0, 1),
    ("rel", 0, 6), ("pre", 3), ("red", 0), ("pre", 1), ("combp", 3), ("rel", 1, 6), ("rel", 1, 3), ("rel", 1, 1),
    ("combp", 1), ("actp", 3), ("act", 0), ("actp", 1), ("rel", 0, 5), ("rel", 0, 2), ("comba", 3), ("sprp", 0),
    ("pre", 2), ("spra", 0), ("comba", 1), ("red", 3), ("rel", 1, 2), ("rel", 0, 4), ("combp", 2), ("grad", 0),
    ("actp", 2), ("pre", 4), ("store", 0), ("join", 0), ("red", 1), ("go", 0), ("rel", 1, 4), ("rel", 1, 5),
    ("comba", 2), ("act", 3), ("gi", 0), ("combp", 4), ("actp", 4), ("act", 1), ("red", 2), ("sprp", 3),
    ("spra", 3), ("rel", 0, 7), ("rel", 1, 7), ("pre", 7), ("comba", 4), ("actp", 7), ("sprp", 1), ("act", 2),
    ("pre", 5), ("actp", 5), ("spra", 1), ("grad", 3), ("store", 3), ("go", 3), ("combp", 7), ("join", 3),
    ("red", 4), ("near0", 1, 0), ("gi", 3), ("comba", 7), ("grad", 1), ("spra", 2), ("gi", 1), ("sprp", 2),
    ("act", 4), ("combp", 5), ("pre", 6), ("actp", 6), ("store", 1), ("join", 1), ("near0", 0, 0), ("go", 1),
    ("comba", 5), ("red", 7), ("store", 2), ("go", 2), ("grad", 2), ("sprp", 4), ("gi", 2), ("spra", 4),
    ("join", 2), ("near0", 0, 1), ("act", 7), ("combp", 6), ("comba", 6), ("red", 5), ("store", 4), ("go", 4),
    ("grad", 4), ("sprp", 7), ("gi", 4), ("spra", 7), ("join", 4), ("act", 5), ("near0", 1, 1), ("red", 6),
    ("grad", 7), ("store", 7), ("go", 7), ("sprp", 5), ("join", 7), ("gi", 7), ("spra", 5), ("act", 6), ("grad", 5),
    ("gi", 5), ("near1", 0, 1), ("sprp", 6), ("near1", 1, 1), ("store", 5), ("join", 5), ("go", 5), ("spra", 6),
    ("grad", 6), ("gi", 6), ("store", 6), ("join", 6), ("xred1",), ("go", 6), ("near1", 0, 0), ("near1", 1, 0),
    ("fin",),
)
SLOT = {where: at for at, where in enumerate(CHUNKS)}
N_CHUNKS = len(CHUNKS)
N_MESSAGES = 192


def gelu_parts(values):
    inner = GELU_SCALE * (values + GELU_CUBIC * values * values * values)
    tangent = jnp.tanh(inner)
    result = 0.5 * values * (1.0 + tangent)
    slope = 0.5 * (1.0 + tangent) + 0.5 * values * (1.0 - tangent * tangent) * GELU_SCALE * (
        1.0 + 3.0 * GELU_CUBIC * values * values
    )
    return (result, slope)


def dot_nn(left, right):
    return lax.dot_general(left, right, (((1,), (0,)), ((), ())), preferred_element_type=F32)


def dot_nt(left, right):
    return lax.dot_general(left, right, (((1,), (1,)), ((), ())), preferred_element_type=F32)


def dot_tn(left, right):
    return lax.dot_general(left, right, (((0,), (0,)), ((), ())), preferred_element_type=F32)


def tiles(total, size):
    return [(at, min(size, total - at)) for at in range(0, total, size)]


def exchange_kernel(
    tok_h, win_h, bias, wout_h, og_h,
    gt, gw_in, gw_out, grad_bias,
    win, wout, tok, og, act, pg, part, r1, r2, comb, summed, summed_in,
    g_out, g_in, keep, pair_out, pair_in, x2_out, x2_in, x1_out, x1_in, acc_in, acc_out,
    send_sem, recv_sem, local_sem,
):
    own, dm = tok_h.shape
    ff = win.shape[1]
    piece = 2 * own // 4
    half = dm // 2
    row, col = lax.axis_index("row"), lax.axis_index("col")
    z, yh = row // 2, row % 2
    x, yl, core = col // 4, (col // 2) % 2, col % 2

    def device(z_, yh_, x_, yl_, core_):
        return (z_ * 2 + yh_, (x_ * 2 + yl_) * 2 + core_)

    to_sib = device(z, yh, x, yl, 1 - core)
    to_yl = device(z, yh, x, 1 - yl, core)
    to_yh = device(z, 1 - yh, x, yl, core)
    to_xp, to_xm = device(z, yh, (x + 1) % 4, yl, core), device(z, yh, (x + 3) % 4, yl, core)
    to_zp, to_zm = device((z + 1) % 4, yh, x, yl, core), device((z + 3) % 4, yh, x, yl, core)
    z1, z2, z3 = (z + 1) % 4, (z + 2) % 4, (z + 3) % 4

    def rows(at):
        return pl.ds(pl.multiple_of(at * piece, piece), piece)

    copies = []

    def send(src, dst, target):
        at = len(copies)
        copy = pltpu.make_async_remote_copy(
            src_ref=src, dst_ref=dst, send_sem=send_sem.at[at], recv_sem=recv_sem.at[at],
            device_id=target, device_id_type=MESH,
        )
        copy.start()
        copies.append(copy)
        return copy

    locals_ = []

    def local_copy(src, dst):
        copy = pltpu.make_async_copy(src, dst, local_sem.at[len(locals_)])
        copy.start()
        locals_.append(copy)
        return copy

    barrier = pltpu.get_barrier_semaphore()
    for target in (to_sib, to_yl, to_yh, to_xp, to_xm, to_zp, to_zm):
        pl.semaphore_signal(barrier, inc=1, device_id=target, device_id_type=MESH)

    mine, other = pl.ds(0, own), pl.ds(own, own)
    sources = ((tok_h, tok.at[0, mine]), (win_h, win), (og_h, og.at[0, mine]), (wout_h, wout))
    loads = [local_copy(src, dst) for src, dst in sources]
    pl.semaphore_wait(barrier, 7)

    gather, red, back = {}, {}, {}
    bufs, halves = (tok, og), ((tok_h, tok), (og_h, og))

    def start():
        for a, (src, buf) in enumerate(halves):
            gather[a, 0, "s"] = send(src, buf.at[0, other], to_sib)
            for where, target in (((0, 1), to_yl), ((3, 0), to_xp), ((1, 0), to_xm)):
                k = SLOT[where]
                gather[a, k] = send(src, buf.at[k, mine], target)

    def load():
        for copy in loads:
            copy.wait()

    def relay(a, k):
        gather[a, k].wait_recv()
        buf, (dx, dy) = bufs[a], CHUNKS[k]
        onward = []
        if (dx, dy) == (0, 1):
            onward = [(SLOT[3, 1], to_xp), (SLOT[1, 1], to_xm)]
        elif (a, dx) == (0, 3):
            onward = [(SLOT[2, dy], to_xp)]
        elif (a, dx) == (1, 1):
            onward = [(SLOT[2, dy], to_xm)]
        for to, target in onward:
            gather[a, to] = send(buf.at[k, mine], buf.at[to, mine], target)
        gather[a, k, "s"] = send(buf.at[k, mine], buf.at[k, other], to_sib)

    def partial_pre(k):
        gather[0, k, "s"].wait_recv()
        for at, size in tiles(ff, 256):
            part[k, 0, :, at : at + size] = dot_nn(tok[k], win[:, at : at + size]).astype(BF16)
        red[k, "1p"] = send(part.at[k, 0, rows(z2)], r1.at[k, 0], to_zp)
        red[k, "2pm"] = send(part.at[k, 0, rows(z3)], r2.at[k, 1], to_zm)

    def partial_act(k):
        gather[1, k, "s"].wait_recv()
        for at, size in tiles(ff, 256):
            part[k, 1, :, at : at + size] = dot_nt(og[k], wout[at : at + size, :]).astype(BF16)
        red[k, "1a"] = send(part.at[k, 1, rows(z2)], r1.at[k, 1], to_zm)
        red[k, "2ap"] = send(part.at[k, 1, rows(z1)], r2.at[k, 2], to_zp)

    def combine(k, a, name, at, sent, into, target):
        red[k, name].wait_recv()
        comb[k, a] = (part[k, a, rows(at), :].astype(F32) + r1[k, a].astype(F32)).astype(BF16)
        red[k, sent] = send(comb.at[k, a], r2.at[k, into], target)

    def combine_pre(k):
        combine(k, 0, "1p", z1, "2pp", 0, to_zp)

    def combine_act(k):
        combine(k, 1, "1a", z3, "2am", 3, to_zm)

    def reduce_pair(k):
        for name in ("2pm", "2ap", "2pp", "2am"):
            red[k, name].wait_recv()
        for a in range(2):
            total = part[k, a, rows(z), :].astype(F32) + (r2[k, 2 * a].astype(F32) + r2[k, 2 * a + 1].astype(F32))
            summed[k, a] = total.astype(BF16)
        red[k, "y"] = send(summed.at[k], summed_in.at[k], to_yh)

    def activate(k):
        red[k, "y"].wait_recv()
        pre = summed[k, 0].astype(F32) + summed_in[k, 0].astype(F32) + bias[...].reshape(1, ff)
        act_grad = summed[k, 1].astype(F32) + summed_in[k, 1].astype(F32)
        result, slope = gelu_parts(pre)
        act[k, rows(z), :] = result.astype(BF16)
        pg[k, rows(z), :] = (act_grad * slope).astype(BF16)
        here = rows(z)
        red[k, "gpp"] = send(pg.at[k, here], pg.at[k, here], to_zp)
        red[k, "gpm"] = send(pg.at[k, here], pg.at[k, here], to_zm)
        red[k, "gap"] = send(act.at[k, here], act.at[k, here], to_zp)
        red[k, "gam"] = send(act.at[k, here], act.at[k, here], to_zm)

    def spread_pg(k):
        red[k, "gpm"].wait_recv()
        red[k, "fp"] = send(pg.at[k, rows(z1)], pg.at[k, rows(z1)], to_zm)

    def spread_act(k):
        red[k, "gap"].wait_recv()
        red[k, "fa"] = send(act.at[k, rows(z3)], act.at[k, rows(z3)], to_zp)

    def grad_in(k):
        for name in ("gpp", "fp"):
            red[k, name].wait_recv()
        for at, size in tiles(dm, 256):
            product = dot_nt(pg[k], win[at : at + size, :])
            keep[k, :, at : at + size] = product[:own].astype(BF16)
            g_out[k, :, at : at + size] = product[own:].astype(BF16)
        back[k, "s"] = send(g_out.at[k], g_in.at[k], to_sib)

    def store_act(k):
        for name in ("gam", "fa"):
            red[k, name].wait_recv()

    seen = set()

    def accumulate(acc, left, right, k, strip):
        first = id(acc) not in seen
        seen.add(id(acc))
        width = right.shape[-1]

        def body(i, carry):
            at = pl.ds(pl.multiple_of(i * strip, strip), strip)
            turned = left[k, :, at].T
            for to, size in tiles(width, 256):
                product = dot_nn(turned, right[k, :, to : to + size])
                acc[at, to : to + size] = product if first else acc[at, to : to + size] + product
            return carry

        lax.fori_loop(0, left.shape[-1] // strip, body, 0)

    def weight_out_part(k):
        accumulate(acc_out, act, og, k, 128)
        done["out"] += 1
        if done["out"] == N_CHUNKS:
            local_copy(acc_out, gw_out)

    def weight_in_part(k):
        accumulate(acc_in, tok, pg, k, 128)
        column = jnp.sum(pg[k].astype(F32), axis=0)
        grad_bias[...] = column if done["in"] == 0 else grad_bias[...] + column
        done["in"] += 1
        if done["in"] == N_CHUNKS:
            local_copy(acc_in, gw_in)

    done = {"out": 0, "in": 0}
    ways = ((1, to_xp), (3, to_xm))

    def cols(side):
        return pl.ds(side * half, half)

    def join_cores(k):
        back[k, "s"].wait_recv()
        dx, dy = CHUNKS[k]
        total = (keep[k].astype(F32) + g_in[k].astype(F32)).astype(BF16)
        if dx == 2:
            for side, (_, target) in enumerate(ways):
                x2_out[dy, side] = total[:, side * half : (side + 1) * half]
                back["far", side, dy] = send(x2_out.at[dy, side], x2_in.at[dy, side], target)
        else:
            keep[k] = total

    def return_near(way, dy):
        dx, target = ways[way]
        x1_out[dy, way, 1 - way] = keep[SLOT[dx, dy], :, cols(1 - way)]
        back["near", way, 1 - way, dy] = send(x1_out.at[dy, way, 1 - way], x1_in.at[dy, way, 1 - way], target)

    def return_both(way, dy):
        dx, target = ways[way]
        back["far", way, dy].wait_recv()
        own_part = keep[SLOT[dx, dy], :, cols(way)].astype(F32)
        x1_out[dy, way, way] = (own_part + x2_in[dy, way].astype(F32)).astype(BF16)
        back["near", way, way, dy] = send(x1_out.at[dy, way, way], x1_in.at[dy, way, way], target)

    def from_row(dy, side):
        for way in range(2):
            back["near", way, side, dy].wait_recv()
        both = x1_in[dy, 0, side].astype(F32) + x1_in[dy, 1, side].astype(F32)
        return keep[SLOT[0, dy], :, cols(side)].astype(F32) + both

    def pass_pair():
        for side in range(2):
            pair_out[:, cols(side)] = from_row(1, side).astype(BF16)
        back["y"] = send(pair_out, pair_in, to_yl)

    def finish():
        back["y"].wait_recv()
        for side in range(2):
            total = from_row(0, side) + pair_in[:, cols(side)].astype(F32)
            gt[:, side * half : (side + 1) * half] = total.astype(BF16)

    stages = {
        "start": start, "load": load, "rel": relay, "pre": partial_pre, "actp": partial_act,
        "combp": combine_pre, "comba": combine_act, "red": reduce_pair, "act": activate,
        "sprp": spread_pg, "spra": spread_act, "grad": grad_in, "store": store_act, "join": join_cores,
        "near0": return_near, "near1": return_both, "xred1": pass_pair, "fin": finish,
        "go": weight_out_part, "gi": weight_in_part,
    }
    for stage, *where in SCHEDULE:
        stages[stage](*where)
    for copy in copies:
        copy.wait_send()
    for copy in locals_[len(loads) :]:
        copy.wait()


def exchange(tokens, weight_in, bias_hidden, weight_out, out_grad):
    own, dm = tokens.shape
    ff = weight_in.shape[1]
    chunk, piece, half = 2 * own, own // 2, dm // 2
    n = N_CHUNKS
    any_space = pl.BlockSpec(memory_space=pl.ANY)
    vmem = pl.BlockSpec(memory_space=pltpu.VMEM)
    flops = 5 * 2 * n * chunk * dm * ff
    return pl.pallas_call(
        exchange_kernel,
        out_shape=(
            jax.ShapeDtypeStruct((own, dm), BF16),
            jax.ShapeDtypeStruct((dm, ff), F32),
            jax.ShapeDtypeStruct((ff, dm), F32),
            jax.ShapeDtypeStruct((ff,), F32),
        ),
        in_specs=[any_space, any_space, vmem, any_space, any_space],
        out_specs=(vmem, any_space, any_space, vmem),
        scratch_shapes=[
            pltpu.VMEM((dm, ff), BF16),
            pltpu.VMEM((ff, dm), BF16),
            pltpu.VMEM((n, chunk, dm), BF16),
            pltpu.VMEM((n, chunk, dm), BF16),
            pltpu.VMEM((n, chunk, ff), BF16),
            pltpu.VMEM((n, chunk, ff), BF16),
            pltpu.VMEM((n, 2, chunk, ff), BF16),
            pltpu.VMEM((n, 2, piece, ff), BF16),
            pltpu.VMEM((n, 4, piece, ff), BF16),
            pltpu.VMEM((n, 2, piece, ff), BF16),
            pltpu.VMEM((n, 2, piece, ff), BF16),
            pltpu.VMEM((n, 2, piece, ff), BF16),
            pltpu.VMEM((n, own, dm), BF16),
            pltpu.VMEM((n, own, dm), BF16),
            pltpu.VMEM((n, own, dm), BF16),
            pltpu.VMEM((own, dm), BF16),
            pltpu.VMEM((own, dm), BF16),
            pltpu.VMEM((2, 2, own, half), BF16),
            pltpu.VMEM((2, 2, own, half), BF16),
            pltpu.VMEM((2, 2, 2, own, half), BF16),
            pltpu.VMEM((2, 2, 2, own, half), BF16),
            pltpu.VMEM((dm, ff), F32),
            pltpu.VMEM((ff, dm), F32),
            pltpu.SemaphoreType.DMA((N_MESSAGES,)),
            pltpu.SemaphoreType.DMA((N_MESSAGES,)),
            pltpu.SemaphoreType.DMA((16,)),
        ],
        compiler_params=pltpu.CompilerParams(
            collective_id=0, has_side_effects=True, vmem_limit_bytes=63 * 1024 * 1024
        ),
        cost_estimate=pl.CostEstimate(flops=flops, bytes_accessed=40_000_000, transcendentals=0),
        name="exchange",
    )(tokens, weight_in, bias_hidden, weight_out, out_grad)


def local(tokens, weight_in, bias_hidden, weight_out, out_grad):
    grad_tokens, grad_weight_in, grad_weight_out, grad_bias = exchange(
        tokens, weight_in, bias_hidden, weight_out, out_grad
    )
    return (grad_tokens, grad_weight_in, grad_bias, grad_weight_out)


def solution(mesh):
    placed = (P("col", "row"), P("row", "col"), P("col"), P("col", "row"), P("col", "row"))
    return jax.shard_map(
        local,
        mesh=mesh,
        in_specs=placed,
        out_specs=(P("col", "row"), P("row", "col"), P("col"), P("col", "row")),
        check_vma=False,
    )
```

```python
import functools

import jax
import jax.numpy as jnp
from jax import lax
from jax.experimental import pallas as pl
from jax.experimental.pallas import tpu as pltpu
from jax.sharding import PartitionSpec as P

GELU_SCALE = 0.7978845608
GELU_CUBIC = 0.044715
MESH = pl.DeviceIdType.MESH
BF16 = jnp.bfloat16
F32 = jnp.float32

CHUNKS = ((0, 0), (3, 0), (1, 0), (1, 1), (2, 0), (2, 1), (3, 1), (0, 1))
SCHEDULE = (
    ("start",), ("load",), ("pre", 0), ("actp", 0), ("combp", 0), ("comba", 0), ("rel", 0, 1), ("rel", 0, 2),
    ("rel", 0, 7), ("pre", 1), ("red", 0), ("combp", 1), ("pre", 2), ("rel", 1, 1), ("rel", 1, 2), ("rel", 1, 7),
    ("actp", 1), ("act", 0), ("actp", 2), ("combp", 2), ("rel", 0, 4), ("rel", 0, 3), ("comba", 1), ("sprp", 0),
    ("pre", 3), ("spra", 0), ("comba", 2), ("red", 1), ("rel", 1, 4), ("rel", 0, 6), ("grad", 0), ("combp", 3),
    ("pre", 4), ("actp", 4), ("store", 0), ("join", 0), ("red", 2), ("gb", 0), ("act", 1), ("rel", 1, 6),
    ("rel", 1, 3), ("combp", 4), ("comba", 4), ("actp", 3), ("sprp", 1), ("act", 2), ("spra", 1), ("rel", 0, 5),
    ("red", 4), ("comba", 3), ("pre", 5), ("rel", 1, 5), ("grad", 1), ("gb", 1), ("actp", 5), ("spra", 2),
    ("sprp", 2), ("join", 1), ("near0", 1, 0), ("act", 4), ("store", 1), ("red", 3), ("combp", 5), ("pre", 6),
    ("actp", 6), ("comba", 5), ("store", 2), ("grad", 2), ("act", 3), ("gb", 2), ("sprp", 4), ("spra", 4),
    ("join", 2), ("near0", 0, 0), ("combp", 6), ("pre", 7), ("comba", 6), ("actp", 7), ("red", 5), ("sprp", 3),
    ("spra", 3), ("store", 4), ("grad", 4), ("act", 5), ("gb", 4), ("combp", 7), ("join", 4), ("red", 6),
    ("comba", 7), ("store", 3), ("go", 0, 3), ("grad", 3), ("go", 1, 3), ("sprp", 5), ("near1", 0, 0), ("act", 6),
    ("spra", 5), ("near1", 1, 0), ("join", 3), ("near0", 0, 1), ("go", 2, 3), ("red", 7), ("gi", 0, 3),
    ("gi", 1, 3), ("grad", 5), ("spra", 6), ("sprp", 6), ("gi", 2, 3), ("fin",), ("gi", 3, 3), ("store", 5),
    ("join", 5), ("act", 7), ("grad", 6), ("store", 6), ("gb", 3), ("go", 0, 5), ("go", 1, 5), ("join", 6),
    ("near0", 1, 1), ("sprp", 7), ("go", 2, 5), ("gi", 0, 5), ("spra", 7), ("near1", 0, 1), ("near1", 1, 1),
    ("gi", 1, 5), ("gi", 2, 5), ("grad", 7), ("gi", 3, 5), ("store", 7), ("gb", 5), ("gb", 6), ("gb", 7),
    ("join", 7), ("xred1",),
)
SLOT = {where: at for at, where in enumerate(CHUNKS)}
N_CHUNKS = len(CHUNKS)
GROUPS = {3: (0, 4), 5: (4, 6)}
LATE = 6
STRIP = 128
OUT_STRIPS = ((0, 2), (2, 4), (4, 7))
IN_STRIPS = ((0, 3), (3, 7), (7, 10), (10, 14))
N_MESSAGES = 192


def gelu_parts(values):
    inner = GELU_SCALE * (values + GELU_CUBIC * values * values * values)
    tangent = jnp.tanh(inner)
    result = 0.5 * values * (1.0 + tangent)
    slope = 0.5 * (1.0 + tangent) + 0.5 * values * (1.0 - tangent * tangent) * GELU_SCALE * (
        1.0 + 3.0 * GELU_CUBIC * values * values
    )
    return (result, slope)


def dot_nn(left, right):
    return lax.dot_general(left, right, (((1,), (0,)), ((), ())), preferred_element_type=F32)


def dot_nt(left, right):
    return lax.dot_general(left, right, (((1,), (1,)), ((), ())), preferred_element_type=F32)


def dot_tn(left, right):
    return lax.dot_general(left, right, (((0,), (0,)), ((), ())), preferred_element_type=F32)


def tiles(total, size):
    return [(at, min(size, total - at)) for at in range(0, total, size)]


def exchange_kernel(
    tok_h, win_h, bias, wout_h, og_h,
    near_sum, pair_out, gw_in, gw_out, grad_bias, act_late, og_late, tok_late, pg_late,
    win, wout, tok, og, act, pg, part, r1, r2, comb, summed, summed_in,
    g_out, g_in, keep, x2_out, x2_in, x1_out, x1_in, acc_in, acc_out,
    send_sem, recv_sem, local_sem,
):
    own, dm = tok_h.shape
    ff = win.shape[1]
    piece = 2 * own // 4
    half = dm // 2
    row, col = lax.axis_index("row"), lax.axis_index("col")
    z, yh = row // 2, row % 2
    x, yl, core = col // 4, (col // 2) % 2, col % 2

    def device(z_, yh_, x_, yl_, core_):
        return (z_ * 2 + yh_, (x_ * 2 + yl_) * 2 + core_)

    to_sib = device(z, yh, x, yl, 1 - core)
    to_yl = device(z, yh, x, 1 - yl, core)
    to_yh = device(z, 1 - yh, x, yl, core)
    to_xp, to_xm = device(z, yh, (x + 1) % 4, yl, core), device(z, yh, (x + 3) % 4, yl, core)
    to_zp, to_zm = device((z + 1) % 4, yh, x, yl, core), device((z + 3) % 4, yh, x, yl, core)
    z1, z2, z3 = (z + 1) % 4, (z + 2) % 4, (z + 3) % 4

    def rows(at):
        return pl.ds(pl.multiple_of(at * piece, piece), piece)

    def late_rows(k):
        return pl.ds((k - LATE) * 2 * own, 2 * own)

    copies = []

    def send(src, dst, target):
        at = len(copies)
        copy = pltpu.make_async_remote_copy(
            src_ref=src, dst_ref=dst, send_sem=send_sem.at[at], recv_sem=recv_sem.at[at],
            device_id=target, device_id_type=MESH,
        )
        copy.start()
        copies.append(copy)
        return copy

    locals_ = []

    def local_copy(src, dst):
        copy = pltpu.make_async_copy(src, dst, local_sem.at[len(locals_)])
        copy.start()
        locals_.append(copy)
        return copy

    barrier = pltpu.get_barrier_semaphore()
    for target in (to_sib, to_yl, to_yh, to_xp, to_xm, to_zp, to_zm):
        pl.semaphore_signal(barrier, inc=1, device_id=target, device_id_type=MESH)

    mine, other = pl.ds(0, own), pl.ds(own, own)
    sources = ((tok_h, tok.at[0, mine]), (win_h, win), (og_h, og.at[0, mine]), (wout_h, wout))
    loads = [local_copy(src, dst) for src, dst in sources]
    pl.semaphore_wait(barrier, 7)

    gather, red, back = {}, {}, {}
    bufs, halves = (tok, og), ((tok_h, tok), (og_h, og))

    def start():
        for a, (src, buf) in enumerate(halves):
            gather[a, 0, "s"] = send(src, buf.at[0, other], to_sib)
            for where, target in (((0, 1), to_yl), ((3, 0), to_xp), ((1, 0), to_xm)):
                k = SLOT[where]
                gather[a, k] = send(src, buf.at[k, mine], target)

    def load():
        for copy in loads:
            copy.wait()

    def relay(a, k):
        gather[a, k].wait_recv()
        buf, (dx, dy) = bufs[a], CHUNKS[k]
        onward = []
        if (dx, dy) == (0, 1):
            onward = [(SLOT[3, 1], to_xp), (SLOT[1, 1], to_xm)]
        elif (a, dx) == (0, 3):
            onward = [(SLOT[2, dy], to_xp)]
        elif (a, dx) == (1, 1):
            onward = [(SLOT[2, dy], to_xm)]
        for to, target in onward:
            gather[a, to] = send(buf.at[k, mine], buf.at[to, mine], target)
        gather[a, k, "s"] = send(buf.at[k, mine], buf.at[k, other], to_sib)

    def partial_pre(k):
        gather[0, k, "s"].wait_recv()
        for at, size in tiles(ff, 256):
            part[k, 0, :, at : at + size] = dot_nn(tok[k], win[:, at : at + size]).astype(BF16)
        red[k, "1p"] = send(part.at[k, 0, rows(z2)], r1.at[k, 0], to_zp)
        red[k, "2pm"] = send(part.at[k, 0, rows(z3)], r2.at[k, 1], to_zm)
        if k >= LATE:
            local_copy(tok.at[k], tok_late.at[late_rows(k)])

    def partial_act(k):
        gather[1, k, "s"].wait_recv()
        for at, size in tiles(ff, 256):
            part[k, 1, :, at : at + size] = dot_nt(og[k], wout[at : at + size, :]).astype(BF16)
        red[k, "1a"] = send(part.at[k, 1, rows(z2)], r1.at[k, 1], to_zm)
        red[k, "2ap"] = send(part.at[k, 1, rows(z1)], r2.at[k, 2], to_zp)
        if k >= LATE:
            local_copy(og.at[k], og_late.at[late_rows(k)])

    def combine(k, a, name, at, sent, into, target):
        red[k, name].wait_recv()
        comb[k, a] = (part[k, a, rows(at), :].astype(F32) + r1[k, a].astype(F32)).astype(BF16)
        red[k, sent] = send(comb.at[k, a], r2.at[k, into], target)

    def combine_pre(k):
        combine(k, 0, "1p", z1, "2pp", 0, to_zp)

    def combine_act(k):
        combine(k, 1, "1a", z3, "2am", 3, to_zm)

    def reduce_pair(k):
        for name in ("2pm", "2ap", "2pp", "2am"):
            red[k, name].wait_recv()
        for a in range(2):
            total = part[k, a, rows(z), :].astype(F32) + (r2[k, 2 * a].astype(F32) + r2[k, 2 * a + 1].astype(F32))
            summed[k, a] = total.astype(BF16)
        red[k, "y"] = send(summed.at[k], summed_in.at[k], to_yh)

    def activate(k):
        red[k, "y"].wait_recv()
        pre = summed[k, 0].astype(F32) + summed_in[k, 0].astype(F32) + bias[...].reshape(1, ff)
        act_grad = summed[k, 1].astype(F32) + summed_in[k, 1].astype(F32)
        result, slope = gelu_parts(pre)
        act[k, rows(z), :] = result.astype(BF16)
        pg[k, rows(z), :] = (act_grad * slope).astype(BF16)
        here = rows(z)
        red[k, "gpp"] = send(pg.at[k, here], pg.at[k, here], to_zp)
        red[k, "gpm"] = send(pg.at[k, here], pg.at[k, here], to_zm)
        red[k, "gap"] = send(act.at[k, here], act.at[k, here], to_zp)
        red[k, "gam"] = send(act.at[k, here], act.at[k, here], to_zm)

    def spread_pg(k):
        red[k, "gpm"].wait_recv()
        red[k, "fp"] = send(pg.at[k, rows(z1)], pg.at[k, rows(z1)], to_zm)

    def spread_act(k):
        red[k, "gap"].wait_recv()
        red[k, "fa"] = send(act.at[k, rows(z3)], act.at[k, rows(z3)], to_zp)

    def grad_in(k):
        for name in ("gpp", "fp"):
            red[k, name].wait_recv()
        if k >= LATE:
            local_copy(pg.at[k], pg_late.at[late_rows(k)])
        for at, size in tiles(dm, 256):
            product = dot_nt(pg[k], win[at : at + size, :])
            keep[k, :, at : at + size] = product[:own].astype(BF16)
            g_out[k, :, at : at + size] = product[own:].astype(BF16)
        back[k, "s"] = send(g_out.at[k], g_in.at[k], to_sib)

    def store_act(k):
        for name in ("gam", "fa"):
            red[k, name].wait_recv()
        if k >= LATE:
            local_copy(act.at[k], act_late.at[late_rows(k)])

    started, done = set(), {"in": 0, "out": 0, "bias": 0}

    def accumulate(acc, left, right, k, strips):
        first = (id(acc), strips) not in started
        started.add((id(acc), strips))
        group = pl.ds(GROUPS[k][0], GROUPS[k][1] - GROUPS[k][0])
        depth = (GROUPS[k][1] - GROUPS[k][0]) * 2 * own

        def body(i, carry):
            at = pl.ds(pl.multiple_of(i * STRIP, STRIP), STRIP)
            turned = left[group, :, at].reshape(depth, STRIP).T
            for to, size in tiles(right.shape[-1], 256):
                product = dot_nn(turned, right[group, :, to : to + size].reshape(depth, size))
                acc[at, to : to + size] = product if first else acc[at, to : to + size] + product
            return carry

        lax.fori_loop(*strips, body, 0)

    def weight_out_part(at, k):
        accumulate(acc_out, act, og, k, OUT_STRIPS[at])
        done["out"] += 1
        if done["out"] == len(GROUPS) * len(OUT_STRIPS):
            local_copy(acc_out, gw_out)

    def weight_in_part(at, k):
        accumulate(acc_in, tok, pg, k, IN_STRIPS[at])
        done["in"] += 1
        if done["in"] == len(GROUPS) * len(IN_STRIPS):
            local_copy(acc_in, gw_in)

    def bias_part(k):
        column = jnp.sum(pg[k].astype(F32), axis=0)
        grad_bias[...] = grad_bias[...] + column if done["bias"] else column
        done["bias"] += 1

    ways = ((1, to_xp), (3, to_xm))

    def cols(side):
        return pl.ds(side * half, half)

    def join_cores(k):
        back[k, "s"].wait_recv()
        dx, dy = CHUNKS[k]
        total = (keep[k].astype(F32) + g_in[k].astype(F32)).astype(BF16)
        if dx == 2:
            for side, (_, target) in enumerate(ways):
                x2_out[dy, side] = total[:, side * half : (side + 1) * half]
                back["far", side, dy] = send(x2_out.at[dy, side], x2_in.at[dy, side], target)
        else:
            keep[k] = total

    def return_near(way, dy):
        dx, target = ways[way]
        x1_out[dy, way, 1 - way] = keep[SLOT[dx, dy], :, cols(1 - way)]
        back["near", way, 1 - way, dy] = send(x1_out.at[dy, way, 1 - way], x1_in.at[dy, way, 1 - way], target)

    def return_both(way, dy):
        dx, target = ways[way]
        back["far", way, dy].wait_recv()
        own_part = keep[SLOT[dx, dy], :, cols(way)].astype(F32)
        x1_out[dy, way, way] = (own_part + x2_in[dy, way].astype(F32)).astype(BF16)
        back["near", way, way, dy] = send(x1_out.at[dy, way, way], x1_in.at[dy, way, way], target)

    def from_row(dy, side):
        for way in range(2):
            back["near", way, side, dy].wait_recv()
        both = x1_in[dy, 0, side].astype(F32) + x1_in[dy, 1, side].astype(F32)
        return keep[SLOT[0, dy], :, cols(side)].astype(F32) + both

    def pass_pair():
        for side in range(2):
            pair_out[:, cols(side)] = from_row(1, side).astype(BF16)

    def finish():
        for side in range(2):
            near_sum[:, cols(side)] = from_row(0, side)

    stages = {
        "start": start, "load": load, "rel": relay, "pre": partial_pre, "actp": partial_act,
        "combp": combine_pre, "comba": combine_act, "red": reduce_pair, "act": activate,
        "sprp": spread_pg, "spra": spread_act, "grad": grad_in, "store": store_act, "join": join_cores,
        "near0": return_near, "near1": return_both, "xred1": pass_pair, "fin": finish,
        "go": weight_out_part, "gi": weight_in_part, "gb": bias_part,
    }
    for stage, *where in SCHEDULE:
        stages[stage](*where)
    for copy in copies:
        copy.wait_send()
    for copy in locals_[len(loads) :]:
        copy.wait()


def exchange(tokens, weight_in, bias_hidden, weight_out, out_grad):
    own, dm = tokens.shape
    ff = weight_in.shape[1]
    chunk, piece, half = 2 * own, own // 2, dm // 2
    n = N_CHUNKS
    late = (n - LATE) * chunk
    any_space = pl.BlockSpec(memory_space=pl.ANY)
    vmem = pl.BlockSpec(memory_space=pltpu.VMEM)
    flops = 5 * 2 * n * chunk * dm * ff
    return pl.pallas_call(
        exchange_kernel,
        out_shape=(
            jax.ShapeDtypeStruct((own, dm), F32),
            jax.ShapeDtypeStruct((own, dm), BF16),
            jax.ShapeDtypeStruct((dm, ff), F32),
            jax.ShapeDtypeStruct((ff, dm), F32),
            jax.ShapeDtypeStruct((ff,), F32),
            jax.ShapeDtypeStruct((late, ff), BF16),
            jax.ShapeDtypeStruct((late, dm), BF16),
            jax.ShapeDtypeStruct((late, dm), BF16),
            jax.ShapeDtypeStruct((late, ff), BF16),
        ),
        in_specs=[any_space, any_space, vmem, any_space, any_space],
        out_specs=(vmem, vmem, any_space, any_space, vmem, *[any_space] * 4),
        scratch_shapes=[
            pltpu.VMEM((dm, ff), BF16),
            pltpu.VMEM((ff, dm), BF16),
            pltpu.VMEM((n, chunk, dm), BF16),
            pltpu.VMEM((n, chunk, dm), BF16),
            pltpu.VMEM((n, chunk, ff), BF16),
            pltpu.VMEM((n, chunk, ff), BF16),
            pltpu.VMEM((n, 2, chunk, ff), BF16),
            pltpu.VMEM((n, 2, piece, ff), BF16),
            pltpu.VMEM((n, 4, piece, ff), BF16),
            pltpu.VMEM((n, 2, piece, ff), BF16),
            pltpu.VMEM((n, 2, piece, ff), BF16),
            pltpu.VMEM((n, 2, piece, ff), BF16),
            pltpu.VMEM((n, own, dm), BF16),
            pltpu.VMEM((n, own, dm), BF16),
            pltpu.VMEM((n, own, dm), BF16),
            pltpu.VMEM((2, 2, own, half), BF16),
            pltpu.VMEM((2, 2, own, half), BF16),
            pltpu.VMEM((2, 2, 2, own, half), BF16),
            pltpu.VMEM((2, 2, 2, own, half), BF16),
            pltpu.VMEM((dm, ff), F32),
            pltpu.VMEM((ff, dm), F32),
            pltpu.SemaphoreType.DMA((N_MESSAGES,)),
            pltpu.SemaphoreType.DMA((N_MESSAGES,)),
            pltpu.SemaphoreType.DMA((24,)),
        ],
        compiler_params=pltpu.CompilerParams(
            collective_id=0, has_side_effects=True, vmem_limit_bytes=63 * 1024 * 1024
        ),
        cost_estimate=pl.CostEstimate(flops=flops, bytes_accessed=40_000_000, transcendentals=0),
        name="exchange",
    )(tokens, weight_in, bias_hidden, weight_out, out_grad)


def settle_kernel(strip, *refs):
    sources, (gw_in, gw_out, bias_o), stops, (in_sem, out_sem) = refs[:7], refs[7:10], refs[10:17], refs[17:]
    sum_in, sum_out, bias, act, og, tok, pg = stops
    started = []

    def fetch(i, here=None):
        src, dst = (sources[i], stops[i]) if here is None else (sources[i].at[here], stops[i].at[here])
        copy = pltpu.make_async_copy(src, dst, in_sem.at[len(started)])
        copy.start()
        started.append(copy)
        return copy

    small = [fetch(i) for i in (3, 4)]
    plan = [(1, sum_out, act, og, gw_out, at) for at in range(0, sum_out.shape[0], strip)]
    fetched = [fetch(i, pl.ds(at, strip)) for i, *_, at in plan]
    more = [fetch(i) for i in (5, 6, 2)]
    plan_in = [(0, sum_in, tok, pg, gw_in, at) for at in range(0, sum_in.shape[0], strip)]
    fetched += [fetch(i, pl.ds(at, strip)) for i, *_, at in plan_in]
    onward = []

    def give(src, dst):
        copy = pltpu.make_async_copy(src, dst, out_sem.at[len(onward)])
        copy.start()
        onward.append(copy)

    for copy in small:
        copy.wait()
    for step, (_, total, left, right, target, at) in enumerate(plan + plan_in):
        if step == len(plan):
            for copy in more:
                copy.wait()
            give(bias, bias_o)
        fetched[step].wait()
        turned = left[:, at : at + strip].T
        for to, size in tiles(right.shape[1], 256):
            total[at : at + strip, to : to + size] += dot_nn(turned, right[:, to : to + size])
        give(total.at[pl.ds(at, strip)], target.at[pl.ds(at, strip)])
    for copy in onward:
        copy.wait()


def settle(*parts):
    any_space = pl.BlockSpec(memory_space=pl.ANY)
    results = parts[:3]
    strip = STRIP
    n = sum(array.shape[0] // strip for array in results[:2]) + 5
    return pl.pallas_call(
        functools.partial(settle_kernel, strip),
        out_shape=tuple(jax.ShapeDtypeStruct(array.shape, array.dtype) for array in results),
        in_specs=[any_space] * len(parts),
        out_specs=(any_space,) * len(results),
        scratch_shapes=[pltpu.VMEM(array.shape, array.dtype) for array in parts]
        + [pltpu.SemaphoreType.DMA((n,))] * 2,
        compiler_params=pltpu.CompilerParams(vmem_limit_bytes=60 * 1024 * 1024),
        cost_estimate=pl.CostEstimate(flops=2_400_000_000, bytes_accessed=28_000_000, transcendentals=0),
        name="settle",
    )(*parts)


def local(tokens, weight_in, bias_hidden, weight_out, out_grad):
    near_sum, for_pair, *rest = exchange(tokens, weight_in, bias_hidden, weight_out, out_grad)
    from_pair = lax.ppermute(for_pair, "col", [(c, c ^ 2) for c in range(16)])
    grad_weight_in, grad_weight_out, grad_bias = settle(*rest)
    grad_tokens = (near_sum + from_pair.astype(F32)).astype(BF16)
    return (grad_tokens, grad_weight_in, grad_bias, grad_weight_out)


def solution(mesh):
    placed = (P("col", "row"), P("row", "col"), P("col"), P("col", "row"), P("col", "row"))
    return jax.shard_map(
        local,
        mesh=mesh,
        in_specs=placed,
        out_specs=(P("col", "row"), P("row", "col"), P("col"), P("col", "row")),
        check_vma=False,
    )
```

```python
import functools

import jax
import jax.numpy as jnp
from jax import lax
from jax.experimental import pallas as pl
from jax.experimental.pallas import tpu as pltpu
from jax.sharding import PartitionSpec as P

GELU_SCALE = 0.7978845608
GELU_CUBIC = 0.044715
MESH = pl.DeviceIdType.MESH
BF16 = jnp.bfloat16
F32 = jnp.float32

CHUNKS = ((0, 0), (3, 0), (2, 0), (1, 0), (1, 1), (2, 1), (0, 1), (3, 1))
SCHEDULE = (
    ("start",), ("load",), ("pre", 0), ("actp", 0), ("combp", 0), ("comba", 0), ("rel", 0, 1), ("rel", 0, 3),
    ("rel", 0, 6), ("pre", 1), ("red", 0), ("pre", 3), ("combp", 1), ("rel", 1, 6), ("rel", 1, 1), ("rel", 1, 3),
    ("combp", 3), ("actp", 1), ("act", 0), ("actp", 3), ("rel", 0, 2), ("rel", 0, 4), ("comba", 1), ("sprp", 0),
    ("pre", 2), ("pre", 4), ("spra", 0), ("comba", 3), ("red", 1), ("rel", 1, 4), ("rel", 0, 7), ("combp", 2),
    ("grad", 0), ("actp", 4), ("combp", 4), ("store", 0), ("gb", 0), ("join", 0), ("act", 1), ("red", 3),
    ("rel", 1, 7), ("rel", 1, 2), ("comba", 4), ("actp", 2), ("sprp", 1), ("spra", 1), ("act", 3), ("red", 4),
    ("rel", 0, 5), ("rel", 1, 5), ("comba", 2), ("store", 1), ("pre", 5), ("grad", 1), ("actp", 5), ("sprp", 3),
    ("pre", 7), ("spra", 3), ("act", 4), ("join", 1), ("combp", 5), ("near0", 1, 0), ("actp", 7), ("red", 2),
    ("gb", 1), ("combp", 7), ("comba", 5), ("store", 3), ("grad", 3), ("gb", 3), ("act", 2), ("spra", 4),
    ("join", 3), ("near0", 0, 0), ("sprp", 4), ("comba", 7), ("red", 5), ("sprp", 2), ("pre", 6), ("spra", 2),
    ("actp", 6), ("store", 4), ("grad", 4), ("act", 5), ("combp", 6), ("red", 7), ("gb", 4), ("join", 4),
    ("near0", 0, 1), ("store", 2), ("grad", 2), ("gb", 2), ("go", 0, 3), ("go", 1, 3), ("comba", 6), ("join", 2),
    ("go", 2, 3), ("spra", 5), ("sprp", 5), ("act", 7), ("gi", 0, 3), ("gi", 1, 3), ("gi", 2, 3), ("red", 6),
    ("store", 5), ("gi", 3, 3), ("grad", 5), ("near1", 0, 0), ("near1", 1, 0), ("go", 0, 5), ("spra", 7),
    ("sprp", 7), ("go", 1, 5), ("join", 5), ("go", 2, 5), ("gi", 0, 5), ("act", 6), ("grad", 7), ("fin",),
    ("store", 7), ("gi", 1, 5), ("gi", 2, 5), ("join", 7), ("near0", 1, 1), ("sprp", 6), ("gi", 3, 5),
    ("near1", 0, 1), ("near1", 1, 1), ("gb", 5), ("spra", 6), ("gb", 7), ("grad", 6), ("gb", 6), ("store", 6),
    ("join", 6), ("xred1",),
)
SLOT = {where: at for at, where in enumerate(CHUNKS)}
N_CHUNKS = len(CHUNKS)
GROUPS = {3: (0, 4), 5: (4, 6)}
LATE = 6
OUT_STRIP, OUT_STRIPS = 128, ((0, 2), (2, 4), (4, 7))
IN_STRIP, IN_STRIPS = 256, ((0, 2), (2, 4), (4, 6), (6, 7))
N_MESSAGES = 192


def gelu_parts(values):
    inner = GELU_SCALE * (values + GELU_CUBIC * values * values * values)
    tangent = jnp.tanh(inner)
    result = 0.5 * values * (1.0 + tangent)
    slope = 0.5 * (1.0 + tangent) + 0.5 * values * (1.0 - tangent * tangent) * GELU_SCALE * (
        1.0 + 3.0 * GELU_CUBIC * values * values
    )
    return (result, slope)


def dot_nn(left, right):
    return lax.dot_general(left, right, (((1,), (0,)), ((), ())), preferred_element_type=F32)


def dot_nt(left, right):
    return lax.dot_general(left, right, (((1,), (1,)), ((), ())), preferred_element_type=F32)


def dot_tn(left, right):
    return lax.dot_general(left, right, (((0,), (0,)), ((), ())), preferred_element_type=F32)


def tiles(total, size):
    return [(at, min(size, total - at)) for at in range(0, total, size)]


def exchange_kernel(
    tok_h, win_h, bias, wout_h, og_h,
    near_sum, pair_out, gw_in, gw_out, grad_bias, act_late, og_late, tok_late, pg_late,
    win, wout, tok, og, act, pg, part, r1, r2, comb, summed, summed_in,
    g_out, g_in, keep, x2_out, x2_in, x1_out, x1_in, acc_in, acc_out,
    send_sem, recv_sem, local_sem,
):
    own, dm = tok_h.shape
    ff = win.shape[1]
    piece = 2 * own // 4
    half = dm // 2
    row, col = lax.axis_index("row"), lax.axis_index("col")
    z, yh = row // 2, row % 2
    x, yl, core = col // 4, (col // 2) % 2, col % 2

    def device(z_, yh_, x_, yl_, core_):
        return (z_ * 2 + yh_, (x_ * 2 + yl_) * 2 + core_)

    to_sib = device(z, yh, x, yl, 1 - core)
    to_yl = device(z, yh, x, 1 - yl, core)
    to_yh = device(z, 1 - yh, x, yl, core)
    to_xp, to_xm = device(z, yh, (x + 1) % 4, yl, core), device(z, yh, (x + 3) % 4, yl, core)
    to_zp, to_zm = device((z + 1) % 4, yh, x, yl, core), device((z + 3) % 4, yh, x, yl, core)
    z1, z2, z3 = (z + 1) % 4, (z + 2) % 4, (z + 3) % 4

    def rows(at):
        return pl.ds(pl.multiple_of(at * piece, piece), piece)

    def late_rows(k):
        return pl.ds((k - LATE) * 2 * own, 2 * own)

    copies = []

    def send(src, dst, target):
        at = len(copies)
        copy = pltpu.make_async_remote_copy(
            src_ref=src, dst_ref=dst, send_sem=send_sem.at[at], recv_sem=recv_sem.at[at],
            device_id=target, device_id_type=MESH,
        )
        copy.start()
        copies.append(copy)
        return copy

    locals_ = []

    def local_copy(src, dst):
        copy = pltpu.make_async_copy(src, dst, local_sem.at[len(locals_)])
        copy.start()
        locals_.append(copy)
        return copy

    barrier = pltpu.get_barrier_semaphore()
    for target in (to_sib, to_yl, to_yh, to_xp, to_xm, to_zp, to_zm):
        pl.semaphore_signal(barrier, inc=1, device_id=target, device_id_type=MESH)

    mine, other = pl.ds(0, own), pl.ds(own, own)
    sources = ((tok_h, tok.at[0, mine]), (win_h, win), (og_h, og.at[0, mine]), (wout_h, wout))
    loads = [local_copy(src, dst) for src, dst in sources]
    pl.semaphore_wait(barrier, 7)

    gather, red, back = {}, {}, {}
    bufs, halves = (tok, og), ((tok_h, tok), (og_h, og))

    def start():
        for a, (src, buf) in enumerate(halves):
            gather[a, 0, "s"] = send(src, buf.at[0, other], to_sib)
            for where, target in (((0, 1), to_yl), ((3, 0), to_xp), ((1, 0), to_xm)):
                k = SLOT[where]
                gather[a, k] = send(src, buf.at[k, mine], target)

    def load():
        for copy in loads:
            copy.wait()

    def relay(a, k):
        gather[a, k].wait_recv()
        buf, (dx, dy) = bufs[a], CHUNKS[k]
        onward = []
        if (dx, dy) == (0, 1):
            onward = [(SLOT[3, 1], to_xp), (SLOT[1, 1], to_xm)]
        elif (a, dx) == (0, 3):
            onward = [(SLOT[2, dy], to_xp)]
        elif (a, dx) == (1, 1):
            onward = [(SLOT[2, dy], to_xm)]
        for to, target in onward:
            gather[a, to] = send(buf.at[k, mine], buf.at[to, mine], target)
        gather[a, k, "s"] = send(buf.at[k, mine], buf.at[k, other], to_sib)

    def partial_pre(k):
        gather[0, k, "s"].wait_recv()
        for at, size in tiles(ff, 256):
            part[k, 0, :, at : at + size] = dot_nn(tok[k], win[:, at : at + size]).astype(BF16)
        red[k, "1p"] = send(part.at[k, 0, rows(z2)], r1.at[k, 0], to_zp)
        red[k, "2pm"] = send(part.at[k, 0, rows(z3)], r2.at[k, 1], to_zm)
        if k >= LATE:
            local_copy(tok.at[k], tok_late.at[late_rows(k)])

    def partial_act(k):
        gather[1, k, "s"].wait_recv()
        for at, size in tiles(ff, 256):
            part[k, 1, :, at : at + size] = dot_nt(og[k], wout[at : at + size, :]).astype(BF16)
        red[k, "1a"] = send(part.at[k, 1, rows(z2)], r1.at[k, 1], to_zm)
        red[k, "2ap"] = send(part.at[k, 1, rows(z1)], r2.at[k, 2], to_zp)
        if k >= LATE:
            local_copy(og.at[k], og_late.at[late_rows(k)])

    def combine(k, a, name, at, sent, into, target):
        red[k, name].wait_recv()
        comb[k, a] = (part[k, a, rows(at), :].astype(F32) + r1[k, a].astype(F32)).astype(BF16)
        red[k, sent] = send(comb.at[k, a], r2.at[k, into], target)

    def combine_pre(k):
        combine(k, 0, "1p", z1, "2pp", 0, to_zp)

    def combine_act(k):
        combine(k, 1, "1a", z3, "2am", 3, to_zm)

    def reduce_pair(k):
        for name in ("2pm", "2ap", "2pp", "2am"):
            red[k, name].wait_recv()
        for a in range(2):
            total = part[k, a, rows(z), :].astype(F32) + (r2[k, 2 * a].astype(F32) + r2[k, 2 * a + 1].astype(F32))
            summed[k, a] = total.astype(BF16)
        red[k, "y"] = send(summed.at[k], summed_in.at[k], to_yh)

    def activate(k):
        red[k, "y"].wait_recv()
        pre = summed[k, 0].astype(F32) + summed_in[k, 0].astype(F32) + bias[...].reshape(1, ff)
        act_grad = summed[k, 1].astype(F32) + summed_in[k, 1].astype(F32)
        result, slope = gelu_parts(pre)
        act[k, rows(z), :] = result.astype(BF16)
        pg[k, rows(z), :] = (act_grad * slope).astype(BF16)
        here = rows(z)
        red[k, "gpp"] = send(pg.at[k, here], pg.at[k, here], to_zp)
        red[k, "gpm"] = send(pg.at[k, here], pg.at[k, here], to_zm)
        red[k, "gap"] = send(act.at[k, here], act.at[k, here], to_zp)
        red[k, "gam"] = send(act.at[k, here], act.at[k, here], to_zm)

    def spread_pg(k):
        red[k, "gpm"].wait_recv()
        red[k, "fp"] = send(pg.at[k, rows(z1)], pg.at[k, rows(z1)], to_zm)

    def spread_act(k):
        red[k, "gap"].wait_recv()
        red[k, "fa"] = send(act.at[k, rows(z3)], act.at[k, rows(z3)], to_zp)

    def grad_in(k):
        for name in ("gpp", "fp"):
            red[k, name].wait_recv()
        if k >= LATE:
            local_copy(pg.at[k], pg_late.at[late_rows(k)])
        for at, size in tiles(dm, 256):
            product = dot_nt(pg[k], win[at : at + size, :])
            keep[k, :, at : at + size] = product[:own].astype(BF16)
            g_out[k, :, at : at + size] = product[own:].astype(BF16)
        back[k, "s"] = send(g_out.at[k], g_in.at[k], to_sib)

    def store_act(k):
        for name in ("gam", "fa"):
            red[k, name].wait_recv()
        if k >= LATE:
            local_copy(act.at[k], act_late.at[late_rows(k)])

    started, done = set(), {"in": 0, "out": 0, "bias": 0}

    def accumulate(acc, left, right, k, strip, strips):
        first = (id(acc), strips) not in started
        started.add((id(acc), strips))
        group = pl.ds(GROUPS[k][0], GROUPS[k][1] - GROUPS[k][0])
        depth = (GROUPS[k][1] - GROUPS[k][0]) * 2 * own

        def body(i, carry):
            at = pl.ds(pl.multiple_of(i * strip, strip), strip)
            turned = left[group, :, at].reshape(depth, strip).T
            for to, size in tiles(right.shape[-1], 256):
                product = dot_nn(turned, right[group, :, to : to + size].reshape(depth, size))
                acc[at, to : to + size] = product if first else acc[at, to : to + size] + product
            return carry

        lax.fori_loop(*strips, body, 0)

    def weight_out_part(at, k):
        accumulate(acc_out, act, og, k, OUT_STRIP, OUT_STRIPS[at])
        done["out"] += 1
        if done["out"] == len(GROUPS) * len(OUT_STRIPS):
            local_copy(acc_out, gw_out)

    def weight_in_part(at, k):
        accumulate(acc_in, tok, pg, k, IN_STRIP, IN_STRIPS[at])
        done["in"] += 1
        if done["in"] == len(GROUPS) * len(IN_STRIPS):
            local_copy(acc_in, gw_in)

    def bias_part(k):
        column = jnp.sum(pg[k].astype(F32), axis=0)
        grad_bias[...] = grad_bias[...] + column if done["bias"] else column
        done["bias"] += 1

    ways = ((1, to_xp), (3, to_xm))

    def cols(side):
        return pl.ds(side * half, half)

    def join_cores(k):
        back[k, "s"].wait_recv()
        dx, dy = CHUNKS[k]
        total = (keep[k].astype(F32) + g_in[k].astype(F32)).astype(BF16)
        if dx == 2:
            for side, (_, target) in enumerate(ways):
                x2_out[dy, side] = total[:, side * half : (side + 1) * half]
                back["far", side, dy] = send(x2_out.at[dy, side], x2_in.at[dy, side], target)
        else:
            keep[k] = total

    def return_near(way, dy):
        dx, target = ways[way]
        x1_out[dy, way, 1 - way] = keep[SLOT[dx, dy], :, cols(1 - way)]
        back["near", way, 1 - way, dy] = send(x1_out.at[dy, way, 1 - way], x1_in.at[dy, way, 1 - way], target)

    def return_both(way, dy):
        dx, target = ways[way]
        back["far", way, dy].wait_recv()
        own_part = keep[SLOT[dx, dy], :, cols(way)].astype(F32)
        x1_out[dy, way, way] = (own_part + x2_in[dy, way].astype(F32)).astype(BF16)
        back["near", way, way, dy] = send(x1_out.at[dy, way, way], x1_in.at[dy, way, way], target)

    def from_row(dy, side):
        for way in range(2):
            back["near", way, side, dy].wait_recv()
        both = x1_in[dy, 0, side].astype(F32) + x1_in[dy, 1, side].astype(F32)
        return keep[SLOT[0, dy], :, cols(side)].astype(F32) + both

    def pass_pair():
        for side in range(2):
            pair_out[:, cols(side)] = from_row(1, side).astype(BF16)

    def finish():
        for side in range(2):
            near_sum[:, cols(side)] = from_row(0, side)

    stages = {
        "start": start, "load": load, "rel": relay, "pre": partial_pre, "actp": partial_act,
        "combp": combine_pre, "comba": combine_act, "red": reduce_pair, "act": activate,
        "sprp": spread_pg, "spra": spread_act, "grad": grad_in, "store": store_act, "join": join_cores,
        "near0": return_near, "near1": return_both, "xred1": pass_pair, "fin": finish,
        "go": weight_out_part, "gi": weight_in_part, "gb": bias_part,
    }
    for stage, *where in SCHEDULE:
        stages[stage](*where)
    for copy in copies:
        copy.wait_send()
    for copy in locals_[len(loads) :]:
        copy.wait()


def exchange(tokens, weight_in, bias_hidden, weight_out, out_grad):
    own, dm = tokens.shape
    ff = weight_in.shape[1]
    chunk, piece, half = 2 * own, own // 2, dm // 2
    n = N_CHUNKS
    late = (n - LATE) * chunk
    any_space = pl.BlockSpec(memory_space=pl.ANY)
    vmem = pl.BlockSpec(memory_space=pltpu.VMEM)
    flops = 5 * 2 * n * chunk * dm * ff
    return pl.pallas_call(
        exchange_kernel,
        out_shape=(
            jax.ShapeDtypeStruct((own, dm), F32),
            jax.ShapeDtypeStruct((own, dm), BF16),
            jax.ShapeDtypeStruct((dm, ff), F32),
            jax.ShapeDtypeStruct((ff, dm), F32),
            jax.ShapeDtypeStruct((ff,), F32),
            jax.ShapeDtypeStruct((late, ff), BF16),
            jax.ShapeDtypeStruct((late, dm), BF16),
            jax.ShapeDtypeStruct((late, dm), BF16),
            jax.ShapeDtypeStruct((late, ff), BF16),
        ),
        in_specs=[any_space, any_space, vmem, any_space, any_space],
        out_specs=(vmem, vmem, any_space, any_space, vmem, *[any_space] * 4),
        scratch_shapes=[
            pltpu.VMEM((dm, ff), BF16),
            pltpu.VMEM((ff, dm), BF16),
            pltpu.VMEM((n, chunk, dm), BF16),
            pltpu.VMEM((n, chunk, dm), BF16),
            pltpu.VMEM((n, chunk, ff), BF16),
            pltpu.VMEM((n, chunk, ff), BF16),
            pltpu.VMEM((n, 2, chunk, ff), BF16),
            pltpu.VMEM((n, 2, piece, ff), BF16),
            pltpu.VMEM((n, 4, piece, ff), BF16),
            pltpu.VMEM((n, 2, piece, ff), BF16),
            pltpu.VMEM((n, 2, piece, ff), BF16),
            pltpu.VMEM((n, 2, piece, ff), BF16),
            pltpu.VMEM((n, own, dm), BF16),
            pltpu.VMEM((n, own, dm), BF16),
            pltpu.VMEM((n, own, dm), BF16),
            pltpu.VMEM((2, 2, own, half), BF16),
            pltpu.VMEM((2, 2, own, half), BF16),
            pltpu.VMEM((2, 2, 2, own, half), BF16),
            pltpu.VMEM((2, 2, 2, own, half), BF16),
            pltpu.VMEM((dm, ff), F32),
            pltpu.VMEM((ff, dm), F32),
            pltpu.SemaphoreType.DMA((N_MESSAGES,)),
            pltpu.SemaphoreType.DMA((N_MESSAGES,)),
            pltpu.SemaphoreType.DMA((24,)),
        ],
        compiler_params=pltpu.CompilerParams(
            collective_id=0, has_side_effects=True, vmem_limit_bytes=63 * 1024 * 1024
        ),
        cost_estimate=pl.CostEstimate(flops=flops, bytes_accessed=40_000_000, transcendentals=0),
        name="exchange",
    )(tokens, weight_in, bias_hidden, weight_out, out_grad)


def settle_kernel(strip, *refs):
    sources, (gw_in, gw_out, bias_o), stops, (in_sem, out_sem) = refs[:7], refs[7:10], refs[10:17], refs[17:]
    sum_in, sum_out, bias, act, og, tok, pg = stops
    started = []

    def fetch(i, here=None):
        src, dst = (sources[i], stops[i]) if here is None else (sources[i].at[here], stops[i].at[here])
        copy = pltpu.make_async_copy(src, dst, in_sem.at[len(started)])
        copy.start()
        started.append(copy)
        return copy

    small = [fetch(i) for i in (3, 4)]
    plan = [(1, sum_out, act, og, gw_out, at) for at in tiles(sum_out.shape[0], strip)]
    fetched = [fetch(i, pl.ds(*at)) for i, *_, at in plan]
    more = [fetch(i) for i in (5, 6, 2)]
    plan_in = [(0, sum_in, tok, pg, gw_in, at) for at in tiles(sum_in.shape[0], strip)]
    fetched += [fetch(i, pl.ds(*at)) for i, *_, at in plan_in]
    onward = []

    def give(src, dst):
        copy = pltpu.make_async_copy(src, dst, out_sem.at[len(onward)])
        copy.start()
        onward.append(copy)

    for copy in small:
        copy.wait()
    for step, (_, total, left, right, target, (at, rows)) in enumerate(plan + plan_in):
        if step == len(plan):
            for copy in more:
                copy.wait()
            give(bias, bias_o)
        fetched[step].wait()
        turned = left[:, at : at + rows].T
        for to, size in tiles(right.shape[1], 256):
            total[at : at + rows, to : to + size] += dot_nn(turned, right[:, to : to + size])
        give(total.at[pl.ds(at, rows)], target.at[pl.ds(at, rows)])
    for copy in onward:
        copy.wait()


def settle(*parts):
    any_space = pl.BlockSpec(memory_space=pl.ANY)
    results = parts[:3]
    strip = 256
    n = sum(len(tiles(array.shape[0], strip)) for array in results[:2]) + 5
    return pl.pallas_call(
        functools.partial(settle_kernel, strip),
        out_shape=tuple(jax.ShapeDtypeStruct(array.shape, array.dtype) for array in results),
        in_specs=[any_space] * len(parts),
        out_specs=(any_space,) * len(results),
        scratch_shapes=[pltpu.VMEM(array.shape, array.dtype) for array in parts]
        + [pltpu.SemaphoreType.DMA((n,))] * 2,
        compiler_params=pltpu.CompilerParams(vmem_limit_bytes=60 * 1024 * 1024),
        cost_estimate=pl.CostEstimate(flops=2_400_000_000, bytes_accessed=28_000_000, transcendentals=0),
        name="settle",
    )(*parts)


def local(tokens, weight_in, bias_hidden, weight_out, out_grad):
    near_sum, for_pair, *rest = exchange(tokens, weight_in, bias_hidden, weight_out, out_grad)
    from_pair = lax.ppermute(for_pair, "col", [(c, c ^ 2) for c in range(16)])
    grad_weight_in, grad_weight_out, grad_bias = settle(*rest)
    grad_tokens = (near_sum + from_pair.astype(F32)).astype(BF16)
    return (grad_tokens, grad_weight_in, grad_bias, grad_weight_out)


def solution(mesh):
    placed = (P("col", "row"), P("row", "col"), P("col"), P("col", "row"), P("col", "row"))
    return jax.shard_map(
        local,
        mesh=mesh,
        in_specs=placed,
        out_specs=(P("col", "row"), P("row", "col"), P("col"), P("col", "row")),
        check_vma=False,
    )
```

```python
import functools

import jax
import jax.numpy as jnp
from jax import lax
from jax.experimental import pallas as pl
from jax.experimental.pallas import tpu as pltpu
from jax.sharding import PartitionSpec as P

GELU_SCALE = 0.7978845608
GELU_CUBIC = 0.044715
MESH = pl.DeviceIdType.MESH
BF16 = jnp.bfloat16
F32 = jnp.float32

CHUNKS = ((0, 0), (3, 0), (2, 0), (1, 0), (1, 1), (2, 1), (0, 1), (3, 1))
SCHEDULE = (
    ("start",), ("load",), ("pre", 0), ("actp", 0), ("combp", 0), ("comba", 0), ("rel", 0, 1), ("rel", 0, 3),
    ("rel", 0, 6), ("pre", 1), ("red", 0), ("pre", 3), ("combp", 1), ("rel", 1, 6), ("rel", 1, 1), ("rel", 1, 3),
    ("combp", 3), ("actp", 1), ("act", 0), ("actp", 3), ("rel", 0, 2), ("rel", 0, 4), ("comba", 1), ("sprp", 0),
    ("pre", 2), ("pre", 4), ("spra", 0), ("comba", 3), ("red", 1), ("rel", 1, 4), ("rel", 0, 7), ("combp", 2),
    ("grad", 0), ("actp", 4), ("combp", 4), ("store", 0), ("gb", 0), ("join", 0), ("act", 1), ("red", 3),
    ("rel", 1, 7), ("rel", 1, 2), ("comba", 4), ("actp", 2), ("sprp", 1), ("spra", 1), ("act", 3), ("red", 4),
    ("rel", 0, 5), ("rel", 1, 5), ("comba", 2), ("store", 1), ("pre", 5), ("grad", 1), ("actp", 5), ("sprp", 3),
    ("pre", 7), ("spra", 3), ("act", 4), ("join", 1), ("combp", 5), ("near0", 1, 0), ("actp", 7), ("red", 2),
    ("gb", 1), ("combp", 7), ("comba", 5), ("store", 3), ("grad", 3), ("gb", 3), ("act", 2), ("spra", 4),
    ("join", 3), ("near0", 0, 0), ("sprp", 4), ("comba", 7), ("red", 5), ("sprp", 2), ("pre", 6), ("spra", 2),
    ("actp", 6), ("store", 4), ("grad", 4), ("act", 5), ("combp", 6), ("red", 7), ("gb", 4), ("join", 4),
    ("near0", 0, 1), ("store", 2), ("grad", 2), ("gb", 2), ("go", 0, 3), ("go", 1, 3), ("comba", 6), ("join", 2),
    ("go", 2, 3), ("spra", 5), ("sprp", 5), ("act", 7), ("gi", 0, 3), ("gi", 1, 3), ("gi", 2, 3), ("red", 6),
    ("store", 5), ("gi", 3, 3), ("grad", 5), ("near1", 0, 0), ("near1", 1, 0), ("go", 0, 5), ("spra", 7),
    ("sprp", 7), ("go", 1, 5), ("join", 5), ("go", 2, 5), ("gi", 0, 5), ("act", 6), ("grad", 7), ("fin",),
    ("store", 7), ("gi", 1, 5), ("gi", 2, 5), ("join", 7), ("near0", 1, 1), ("sprp", 6), ("gi", 3, 5),
    ("near1", 0, 1), ("near1", 1, 1), ("gb", 5), ("spra", 6), ("gb", 7), ("grad", 6), ("gb", 6), ("store", 6),
    ("join", 6), ("xred1",),
)
SLOT = {where: at for at, where in enumerate(CHUNKS)}
N_CHUNKS = len(CHUNKS)
GROUPS = {3: (0, 4), 5: (4, 6)}
LATE = 6
OUT_STRIPS = (((256, (0, 1)),), ((256, (1, 2)),), ((256, (2, 3)), (128, (6, 7))))
IN_STRIP, IN_STRIPS = 256, ((0, 2), (2, 4), (4, 6), (6, 7))
N_MESSAGES = 192


def gelu_parts(values):
    inner = GELU_SCALE * (values + GELU_CUBIC * values * values * values)
    tangent = jnp.tanh(inner)
    result = 0.5 * values * (1.0 + tangent)
    slope = 0.5 * (1.0 + tangent) + 0.5 * values * (1.0 - tangent * tangent) * GELU_SCALE * (
        1.0 + 3.0 * GELU_CUBIC * values * values
    )
    return (result, slope)


def dot_nn(left, right):
    return lax.dot_general(left, right, (((1,), (0,)), ((), ())), preferred_element_type=F32)


def dot_nt(left, right):
    return lax.dot_general(left, right, (((1,), (1,)), ((), ())), preferred_element_type=F32)


def dot_tn(left, right):
    return lax.dot_general(left, right, (((0,), (0,)), ((), ())), preferred_element_type=F32)


def tiles(total, size):
    return [(at, min(size, total - at)) for at in range(0, total, size)]


def exchange_kernel(
    tok_h, win_h, bias, wout_h, og_h,
    near_sum, pair_out, gw_in, gw_out, grad_bias, act_late, og_late, tok_late, pg_late,
    win, wout, tok, og, act, pg, part, r1, r2, comb, summed, summed_in,
    g_out, g_in, keep, x2_out, x2_in, x1_out, x1_in, acc_in, acc_out,
    send_sem, recv_sem, local_sem,
):
    own, dm = tok_h.shape
    ff = win.shape[1]
    piece = 2 * own // 4
    half = dm // 2
    row, col = lax.axis_index("row"), lax.axis_index("col")
    z, yh = row // 2, row % 2
    x, yl, core = col // 4, (col // 2) % 2, col % 2

    def device(z_, yh_, x_, yl_, core_):
        return (z_ * 2 + yh_, (x_ * 2 + yl_) * 2 + core_)

    to_sib = device(z, yh, x, yl, 1 - core)
    to_yl = device(z, yh, x, 1 - yl, core)
    to_yh = device(z, 1 - yh, x, yl, core)
    to_xp, to_xm = device(z, yh, (x + 1) % 4, yl, core), device(z, yh, (x + 3) % 4, yl, core)
    to_zp, to_zm = device((z + 1) % 4, yh, x, yl, core), device((z + 3) % 4, yh, x, yl, core)
    z1, z2, z3 = (z + 1) % 4, (z + 2) % 4, (z + 3) % 4

    def rows(at):
        return pl.ds(pl.multiple_of(at * piece, piece), piece)

    def late_rows(k):
        return pl.ds((k - LATE) * 2 * own, 2 * own)

    copies = []

    def send(src, dst, target):
        at = len(copies)
        copy = pltpu.make_async_remote_copy(
            src_ref=src, dst_ref=dst, send_sem=send_sem.at[at], recv_sem=recv_sem.at[at],
            device_id=target, device_id_type=MESH,
        )
        copy.start()
        copies.append(copy)
        return copy

    locals_ = []

    def local_copy(src, dst):
        copy = pltpu.make_async_copy(src, dst, local_sem.at[len(locals_)])
        copy.start()
        locals_.append(copy)
        return copy

    barrier = pltpu.get_barrier_semaphore()
    for target in (to_sib, to_yl, to_yh, to_xp, to_xm, to_zp, to_zm):
        pl.semaphore_signal(barrier, inc=1, device_id=target, device_id_type=MESH)

    mine, other = pl.ds(0, own), pl.ds(own, own)
    sources = ((tok_h, tok.at[0, mine]), (win_h, win), (og_h, og.at[0, mine]), (wout_h, wout))
    loads = [local_copy(src, dst) for src, dst in sources]
    pl.semaphore_wait(barrier, 7)

    gather, red, back = {}, {}, {}
    bufs, halves = (tok, og), ((tok_h, tok), (og_h, og))

    def start():
        for a, (src, buf) in enumerate(halves):
            gather[a, 0, "s"] = send(src, buf.at[0, other], to_sib)
            for where, target in (((0, 1), to_yl), ((3, 0), to_xp), ((1, 0), to_xm)):
                k = SLOT[where]
                gather[a, k] = send(src, buf.at[k, mine], target)

    def load():
        for copy in loads:
            copy.wait()

    def relay(a, k):
        gather[a, k].wait_recv()
        buf, (dx, dy) = bufs[a], CHUNKS[k]
        onward = []
        if (dx, dy) == (0, 1):
            onward = [(SLOT[3, 1], to_xp), (SLOT[1, 1], to_xm)]
        elif (a, dx) == (0, 3):
            onward = [(SLOT[2, dy], to_xp)]
        elif (a, dx) == (1, 1):
            onward = [(SLOT[2, dy], to_xm)]
        for to, target in onward:
            gather[a, to] = send(buf.at[k, mine], buf.at[to, mine], target)
        gather[a, k, "s"] = send(buf.at[k, mine], buf.at[k, other], to_sib)

    def partial_pre(k):
        gather[0, k, "s"].wait_recv()
        for at, size in tiles(ff, 256):
            part[k, 0, :, at : at + size] = dot_nn(tok[k], win[:, at : at + size]).astype(BF16)
        red[k, "1p"] = send(part.at[k, 0, rows(z2)], r1.at[k, 0], to_zp)
        red[k, "2pm"] = send(part.at[k, 0, rows(z3)], r2.at[k, 1], to_zm)
        if k >= LATE:
            local_copy(tok.at[k], tok_late.at[late_rows(k)])

    def partial_act(k):
        gather[1, k, "s"].wait_recv()
        for at, size in tiles(ff, 256):
            part[k, 1, :, at : at + size] = dot_nt(og[k], wout[at : at + size, :]).astype(BF16)
        red[k, "1a"] = send(part.at[k, 1, rows(z2)], r1.at[k, 1], to_zm)
        red[k, "2ap"] = send(part.at[k, 1, rows(z1)], r2.at[k, 2], to_zp)
        if k >= LATE:
            local_copy(og.at[k], og_late.at[late_rows(k)])

    def combine(k, a, name, at, sent, into, target):
        red[k, name].wait_recv()
        comb[k, a] = (part[k, a, rows(at), :].astype(F32) + r1[k, a].astype(F32)).astype(BF16)
        red[k, sent] = send(comb.at[k, a], r2.at[k, into], target)

    def combine_pre(k):
        combine(k, 0, "1p", z1, "2pp", 0, to_zp)

    def combine_act(k):
        combine(k, 1, "1a", z3, "2am", 3, to_zm)

    def reduce_pair(k):
        for name in ("2pm", "2ap", "2pp", "2am"):
            red[k, name].wait_recv()
        for a in range(2):
            total = part[k, a, rows(z), :].astype(F32) + (r2[k, 2 * a].astype(F32) + r2[k, 2 * a + 1].astype(F32))
            summed[k, a] = total.astype(BF16)
        red[k, "y"] = send(summed.at[k], summed_in.at[k], to_yh)

    def activate(k):
        red[k, "y"].wait_recv()
        pre = summed[k, 0].astype(F32) + summed_in[k, 0].astype(F32) + bias[...].reshape(1, ff)
        act_grad = summed[k, 1].astype(F32) + summed_in[k, 1].astype(F32)
        result, slope = gelu_parts(pre)
        act[k, rows(z), :] = result.astype(BF16)
        pg[k, rows(z), :] = (act_grad * slope).astype(BF16)
        here = rows(z)
        red[k, "gpp"] = send(pg.at[k, here], pg.at[k, here], to_zp)
        red[k, "gpm"] = send(pg.at[k, here], pg.at[k, here], to_zm)
        red[k, "gap"] = send(act.at[k, here], act.at[k, here], to_zp)
        red[k, "gam"] = send(act.at[k, here], act.at[k, here], to_zm)

    def spread_pg(k):
        red[k, "gpm"].wait_recv()
        red[k, "fp"] = send(pg.at[k, rows(z1)], pg.at[k, rows(z1)], to_zm)

    def spread_act(k):
        red[k, "gap"].wait_recv()
        red[k, "fa"] = send(act.at[k, rows(z3)], act.at[k, rows(z3)], to_zp)

    def grad_in(k):
        for name in ("gpp", "fp"):
            red[k, name].wait_recv()
        if k >= LATE:
            local_copy(pg.at[k], pg_late.at[late_rows(k)])
        for at, size in tiles(dm, 256):
            product = dot_nt(pg[k], win[at : at + size, :])
            keep[k, :, at : at + size] = product[:own].astype(BF16)
            g_out[k, :, at : at + size] = product[own:].astype(BF16)
        back[k, "s"] = send(g_out.at[k], g_in.at[k], to_sib)

    def store_act(k):
        for name in ("gam", "fa"):
            red[k, name].wait_recv()
        if k >= LATE:
            local_copy(act.at[k], act_late.at[late_rows(k)])

    started, done = set(), {"in": 0, "out": 0, "bias": 0}

    def accumulate(acc, left, right, k, strip, strips):
        first = (id(acc), strips) not in started
        started.add((id(acc), strips))
        group = pl.ds(GROUPS[k][0], GROUPS[k][1] - GROUPS[k][0])
        depth = (GROUPS[k][1] - GROUPS[k][0]) * 2 * own

        def body(i, carry):
            at = pl.ds(pl.multiple_of(i * strip, strip), strip)
            turned = left[group, :, at].reshape(depth, strip).T
            for to, size in tiles(right.shape[-1], 256):
                product = dot_nn(turned, right[group, :, to : to + size].reshape(depth, size))
                acc[at, to : to + size] = product if first else acc[at, to : to + size] + product
            return carry

        lax.fori_loop(*strips, body, 0)

    def weight_out_part(at, k):
        for strip, strips in OUT_STRIPS[at]:
            accumulate(acc_out, act, og, k, strip, strips)
        done["out"] += 1
        if done["out"] == len(GROUPS) * len(OUT_STRIPS):
            local_copy(acc_out, gw_out)

    def weight_in_part(at, k):
        accumulate(acc_in, tok, pg, k, IN_STRIP, IN_STRIPS[at])
        done["in"] += 1
        if done["in"] == len(GROUPS) * len(IN_STRIPS):
            local_copy(acc_in, gw_in)

    def bias_part(k):
        column = jnp.sum(pg[k].astype(F32), axis=0)
        grad_bias[...] = grad_bias[...] + column if done["bias"] else column
        done["bias"] += 1

    ways = ((1, to_xp), (3, to_xm))

    def cols(side):
        return pl.ds(side * half, half)

    def join_cores(k):
        back[k, "s"].wait_recv()
        dx, dy = CHUNKS[k]
        total = (keep[k].astype(F32) + g_in[k].astype(F32)).astype(BF16)
        if dx == 2:
            for side, (_, target) in enumerate(ways):
                x2_out[dy, side] = total[:, side * half : (side + 1) * half]
                back["far", side, dy] = send(x2_out.at[dy, side], x2_in.at[dy, side], target)
        else:
            keep[k] = total

    def return_near(way, dy):
        dx, target = ways[way]
        x1_out[dy, way, 1 - way] = keep[SLOT[dx, dy], :, cols(1 - way)]
        back["near", way, 1 - way, dy] = send(x1_out.at[dy, way, 1 - way], x1_in.at[dy, way, 1 - way], target)

    def return_both(way, dy):
        dx, target = ways[way]
        back["far", way, dy].wait_recv()
        own_part = keep[SLOT[dx, dy], :, cols(way)].astype(F32)
        x1_out[dy, way, way] = (own_part + x2_in[dy, way].astype(F32)).astype(BF16)
        back["near", way, way, dy] = send(x1_out.at[dy, way, way], x1_in.at[dy, way, way], target)

    def from_row(dy, side):
        for way in range(2):
            back["near", way, side, dy].wait_recv()
        both = x1_in[dy, 0, side].astype(F32) + x1_in[dy, 1, side].astype(F32)
        return keep[SLOT[0, dy], :, cols(side)].astype(F32) + both

    def pass_pair():
        for side in range(2):
            pair_out[:, cols(side)] = from_row(1, side).astype(BF16)

    def finish():
        for side in range(2):
            near_sum[:, cols(side)] = from_row(0, side)

    stages = {
        "start": start, "load": load, "rel": relay, "pre": partial_pre, "actp": partial_act,
        "combp": combine_pre, "comba": combine_act, "red": reduce_pair, "act": activate,
        "sprp": spread_pg, "spra": spread_act, "grad": grad_in, "store": store_act, "join": join_cores,
        "near0": return_near, "near1": return_both, "xred1": pass_pair, "fin": finish,
        "go": weight_out_part, "gi": weight_in_part, "gb": bias_part,
    }
    for stage, *where in SCHEDULE:
        stages[stage](*where)
    for copy in copies:
        copy.wait_send()
    for copy in locals_[len(loads) :]:
        copy.wait()


def exchange(tokens, weight_in, bias_hidden, weight_out, out_grad):
    own, dm = tokens.shape
    ff = weight_in.shape[1]
    chunk, piece, half = 2 * own, own // 2, dm // 2
    n = N_CHUNKS
    late = (n - LATE) * chunk
    any_space = pl.BlockSpec(memory_space=pl.ANY)
    vmem = pl.BlockSpec(memory_space=pltpu.VMEM)
    flops = 5 * 2 * n * chunk * dm * ff
    return pl.pallas_call(
        exchange_kernel,
        out_shape=(
            jax.ShapeDtypeStruct((own, dm), F32),
            jax.ShapeDtypeStruct((own, dm), BF16),
            jax.ShapeDtypeStruct((dm, ff), F32),
            jax.ShapeDtypeStruct((ff, dm), F32),
            jax.ShapeDtypeStruct((ff,), F32),
            jax.ShapeDtypeStruct((late, ff), BF16),
            jax.ShapeDtypeStruct((late, dm), BF16),
            jax.ShapeDtypeStruct((late, dm), BF16),
            jax.ShapeDtypeStruct((late, ff), BF16),
        ),
        in_specs=[any_space, any_space, vmem, any_space, any_space],
        out_specs=(vmem, vmem, any_space, any_space, vmem, *[any_space] * 4),
        scratch_shapes=[
            pltpu.VMEM((dm, ff), BF16),
            pltpu.VMEM((ff, dm), BF16),
            pltpu.VMEM((n, chunk, dm), BF16),
            pltpu.VMEM((n, chunk, dm), BF16),
            pltpu.VMEM((n, chunk, ff), BF16),
            pltpu.VMEM((n, chunk, ff), BF16),
            pltpu.VMEM((n, 2, chunk, ff), BF16),
            pltpu.VMEM((n, 2, piece, ff), BF16),
            pltpu.VMEM((n, 4, piece, ff), BF16),
            pltpu.VMEM((n, 2, piece, ff), BF16),
            pltpu.VMEM((n, 2, piece, ff), BF16),
            pltpu.VMEM((n, 2, piece, ff), BF16),
            pltpu.VMEM((n, own, dm), BF16),
            pltpu.VMEM((n, own, dm), BF16),
            pltpu.VMEM((n, own, dm), BF16),
            pltpu.VMEM((2, 2, own, half), BF16),
            pltpu.VMEM((2, 2, own, half), BF16),
            pltpu.VMEM((2, 2, 2, own, half), BF16),
            pltpu.VMEM((2, 2, 2, own, half), BF16),
            pltpu.VMEM((dm, ff), F32),
            pltpu.VMEM((ff, dm), F32),
            pltpu.SemaphoreType.DMA((N_MESSAGES,)),
            pltpu.SemaphoreType.DMA((N_MESSAGES,)),
            pltpu.SemaphoreType.DMA((24,)),
        ],
        compiler_params=pltpu.CompilerParams(
            collective_id=0, has_side_effects=True, vmem_limit_bytes=63 * 1024 * 1024
        ),
        cost_estimate=pl.CostEstimate(flops=flops, bytes_accessed=40_000_000, transcendentals=0),
        name="exchange",
    )(tokens, weight_in, bias_hidden, weight_out, out_grad)


def settle_kernel(strip, *refs):
    sources, (gw_in, gw_out, bias_o), stops, (in_sem, out_sem) = refs[:7], refs[7:10], refs[10:17], refs[17:]
    sum_in, sum_out, bias, act, og, tok, pg = stops
    started = []

    def fetch(i, here=None):
        src, dst = (sources[i], stops[i]) if here is None else (sources[i].at[here], stops[i].at[here])
        copy = pltpu.make_async_copy(src, dst, in_sem.at[len(started)])
        copy.start()
        started.append(copy)
        return copy

    small = [fetch(i) for i in (3, 4)]
    plan = [(1, sum_out, act, og, gw_out, at) for at in tiles(sum_out.shape[0], strip)]
    fetched = [fetch(i, pl.ds(*at)) for i, *_, at in plan]
    more = [fetch(i) for i in (5, 6, 2)]
    plan_in = [(0, sum_in, tok, pg, gw_in, at) for at in tiles(sum_in.shape[0], strip)]
    fetched += [fetch(i, pl.ds(*at)) for i, *_, at in plan_in]
    onward = []

    def give(src, dst):
        copy = pltpu.make_async_copy(src, dst, out_sem.at[len(onward)])
        copy.start()
        onward.append(copy)

    for copy in small:
        copy.wait()
    for step, (_, total, left, right, target, (at, rows)) in enumerate(plan + plan_in):
        if step == len(plan):
            for copy in more:
                copy.wait()
            give(bias, bias_o)
        fetched[step].wait()
        turned = left[:, at : at + rows].T
        for to, size in tiles(right.shape[1], 256):
            total[at : at + rows, to : to + size] += dot_nn(turned, right[:, to : to + size])
        give(total.at[pl.ds(at, rows)], target.at[pl.ds(at, rows)])
    for copy in onward:
        copy.wait()


def settle(*parts):
    any_space = pl.BlockSpec(memory_space=pl.ANY)
    results = parts[:3]
    strip = 256
    n = sum(len(tiles(array.shape[0], strip)) for array in results[:2]) + 5
    return pl.pallas_call(
        functools.partial(settle_kernel, strip),
        out_shape=tuple(jax.ShapeDtypeStruct(array.shape, array.dtype) for array in results),
        in_specs=[any_space] * len(parts),
        out_specs=(any_space,) * len(results),
        scratch_shapes=[pltpu.VMEM(array.shape, array.dtype) for array in parts]
        + [pltpu.SemaphoreType.DMA((n,))] * 2,
        compiler_params=pltpu.CompilerParams(vmem_limit_bytes=60 * 1024 * 1024),
        cost_estimate=pl.CostEstimate(flops=2_400_000_000, bytes_accessed=28_000_000, transcendentals=0),
        name="settle",
    )(*parts)


def local(tokens, weight_in, bias_hidden, weight_out, out_grad):
    near_sum, for_pair, *rest = exchange(tokens, weight_in, bias_hidden, weight_out, out_grad)
    from_pair = lax.ppermute(for_pair, "col", [(c, c ^ 2) for c in range(16)])
    grad_weight_in, grad_weight_out, grad_bias = settle(*rest)
    grad_tokens = (near_sum + from_pair.astype(F32)).astype(BF16)
    return (grad_tokens, grad_weight_in, grad_bias, grad_weight_out)


def solution(mesh):
    placed = (P("col", "row"), P("row", "col"), P("col"), P("col", "row"), P("col", "row"))
    return jax.shard_map(
        local,
        mesh=mesh,
        in_specs=placed,
        out_specs=(P("col", "row"), P("row", "col"), P("col"), P("col", "row")),
        check_vma=False,
    )
```
